32 devices in a mesh: section: 2 (over y), dp: 16 (over z, x, core).
Axes of the slice: x: 2, y: 2, z: 4, core: 2. Of those that a mesh axis runs over, the one named last changes fastest.
Arguments:
- inputs: bfloat16 [16384, 768], P('dp'), may hold values from -6 to 6
- video_ids: int32 [16384], P('dp'), may hold values from 0 to 63, as said below
- view_ids: int32 [16384], P('dp'), may hold values from 0 to 2, as said below
- attn_gain: float32 [2, 768], P('section'), may hold values from 0.1 to 1.9
- mlp_gain: float32 [2, 768], P('section'), may hold values from 0.1 to 1.9
- w_qkv: bfloat16 [2, 768, 2304], P('section'), may hold values from -0.21875 to 0.21875
- w_proj: bfloat16 [2, 768, 768], P('section'), may hold values from -1.25 to 1.25
- w_up: bfloat16 [2, 768, 3072], P('section'), may hold values from -0.21875 to 0.21875
- w_down: bfloat16 [2, 3072, 768], P('section'), may hold values from -0.109375 to 0.109375
- out_grad: bfloat16 [16384, 768], P('dp'), may hold values from -6 to 6
Outputs:
- layer_outputs: bfloat16 [2, 16384, 768], P('section', 'dp')
- input_grads: bfloat16 [2, 16384, 768], P('section', 'dp')
- grad_attn_gain: float32 [2, 768], P('section', 'dp')
- grad_mlp_gain: float32 [2, 768], P('section', 'dp')
- grad_w_qkv: float32 [2, 768, 2304], P('section', 'dp')
- grad_w_proj: float32 [2, 768, 768], P('section', 'dp')
- grad_w_up: float32 [2, 768, 3072], P('section', 'dp')
- grad_w_down: float32 [2, 3072, 768], P('section', 'dp')
The draws below stay inside these ranges and needn't reach their ends.
Inputs may be any that keep to these rules, and one draw needn't show every extreme that they name: `video_ids`: each aligned block of 512 rows holds two clips, each in consecutive rows: ids 2b and 2b + 1 for block b; each clip has between a quarter and three quarters of the block. `view_ids`: every clip has tokens of all three views; its first three rows hold views 0, 1, 2.
All inputs are finite; a program needn't handle non-finite values.
Results may differ from the reference program's by a relative error of at most 0.023.
Values may be sent and summed in bfloat16 or wider, within the bound.
A program may use at most 192 MiB of HBM per device.

```python
import jax
import jax.numpy as jnp
from jax import lax

D = 768
HEAD_DIM = 64
FF = 3072
MB_ROWS = 512
TOKENS = 16384


def clip_layout(key):
    cut_key, view_key = jax.random.split(jax.random.fold_in(key, 7))
    block_total = TOKENS // MB_ROWS
    cuts = jax.random.randint(cut_key, (block_total, 1), MB_ROWS // 4, 3 * MB_ROWS // 4 + 1)
    position = jnp.arange(MB_ROWS, dtype=jnp.int32)[None, :]
    second = (position >= cuts).astype(jnp.int32)
    video = 2 * jnp.arange(block_total, dtype=jnp.int32)[:, None] + second
    clip_start = jnp.where(second == 1, cuts, 0)
    inside = position - clip_start
    rolled = jax.random.randint(view_key, (block_total, MB_ROWS), 0, 7)
    view = jnp.where(rolled < 4, 0, jnp.where(rolled < 6, 1, 2))
    view = jnp.where(inside < 3, inside, view)
    return (video.reshape(-1).astype(jnp.int32), view.reshape(-1).astype(jnp.int32))


def draw_video_ids(key, part):
    return clip_layout(key)[0]


def draw_view_ids(key, part):
    return clip_layout(key)[1]


def with_spikes(result, key, source, target, shards_of, factor):
    owner, partner = [(jnp.arange(result.shape[dim]) // (result.shape[dim] // shards_of)).reshape([-1 if axis == dim else 1 for axis in range(result.ndim)]) for dim in (source, target)]
    chosen = jax.random.permutation(key, shards_of)[partner]
    strong = (owner == chosen) | (owner == (partner + shards_of // 2) % shards_of)
    return jnp.where(strong, factor * result, result)


def steps_of(key, dims, cuts, least, high):
    def one(axis_at, blocks):
        draws = jax.random.uniform(jax.random.fold_in(jax.random.fold_in(key, 6), axis_at), (blocks,), jnp.float32, least / len(cuts), high / len(cuts))
        return jnp.repeat(jnp.exp(draws), dims[axis_at] // blocks).reshape((-1,) + (1,) * (len(dims) - axis_at - 1))

    gain = one(*cuts[0])
    for cut in cuts[1:]:
        gain = gain * one(*cut)
    return gain


def centred(stream_key, extent, spread, most, cuts=(), held_as=jnp.bfloat16):
    drawn = spread * jax.random.normal(stream_key, extent, jnp.float32)
    if cuts:
        drawn = drawn * steps_of(stream_key, extent, cuts, -0.22, 0.18)
    return jnp.clip(drawn, -most, most).astype(held_as)


def heavy_noise(own_key, shape, width, reach, cuts, heavy, kind=jnp.bfloat16):
    entries = width * jax.random.normal(own_key, shape, jnp.float32)
    if cuts:
        entries = entries * steps_of(own_key, shape, cuts, -0.22, 0.18)
    return jnp.clip(with_spikes(entries, jax.random.fold_in(own_key, 3), *heavy), -reach, reach).astype(kind)


def setup_inputs(seed: int = 0) -> dict:
    key_list = jax.random.split(jax.random.key(seed), 11)
    inputs = heavy_noise(key_list[0], (TOKENS, D), 1.0, 6.0, ((0, 16),), (0, 1, 16, 2.0))
    video_ids = draw_video_ids(jax.random.fold_in(key_list[10], 71), 0)
    view_ids = draw_view_ids(jax.random.fold_in(key_list[10], 71), 0)
    attn_gain = jnp.clip(1.0 + 0.18 * jax.random.normal(key_list[3], (2, D), jnp.float32), 0.1, 1.9)
    mlp_gain = jnp.clip(1.0 + 0.18 * jax.random.normal(key_list[4], (2, D), jnp.float32), 0.1, 1.9)
    w_qkv = centred(key_list[5], (2, D, 3 * D), D ** -0.5, 0.21875, ((0, 2),))
    w_proj = centred(key_list[6], (2, D, D), (D // 32) ** -0.5, 1.25, ((0, 2),))
    w_up = centred(key_list[7], (2, D, FF), D ** -0.5, 0.21875, ((0, 2),))
    w_down = centred(key_list[8], (2, FF, D), FF ** -0.5, 0.109375, ((0, 2),))
    out_grad = centred(key_list[9], (TOKENS, D), 1.0, 6.0, ((0, 16),))
    return dict(inputs=inputs, video_ids=video_ids, view_ids=view_ids, attn_gain=attn_gain, mlp_gain=mlp_gain, w_qkv=w_qkv, w_proj=w_proj, w_up=w_up, w_down=w_down, out_grad=out_grad)


@jax.custom_vjp
def low(v):
    return lax.optimization_barrier(v.astype(jnp.bfloat16)).astype(jnp.float32)

@jax.custom_vjp
def low_back(v):
    return v

def low_keep(v):
    return (low(v), None)

def low_pass(kept, grad):
    return (grad,)

def back_keep(v):
    return (v, None)

def back_low(kept, grad):
    return (low(grad),)
low.defvjp(low_keep, low_pass)
low_back.defvjp(back_keep, back_low)
EPSILON = 1e-06
NEG_FILL = -1e+30
HIGHEST = lax.Precision.HIGHEST

def layer_norm(values, gain_row):
    center = values - lax.optimization_barrier(jnp.mean(values, axis=-1, keepdims=True))
    inv_scale = lax.rsqrt(lax.optimization_barrier(jnp.mean(center * center, axis=-1, keepdims=True)) + EPSILON)
    return center * inv_scale * gain_row

def matmul(left, right):
    return jnp.dot(left, right, precision=HIGHEST, preferred_element_type=jnp.float32)

def block_forward(layer_in, video_rows, view_rows, offset, params):
    attn_gain, mlp_gain, w_qkv, w_proj, w_up, w_down = params
    row_count, model_width = layer_in.shape
    head_count = model_width // HEAD_DIM
    normed_attn = low(layer_norm(layer_in, attn_gain))
    qkv_rows = low_back(low(matmul(normed_attn, w_qkv)))
    qkv_split = qkv_rows.reshape(row_count, 3, head_count, HEAD_DIM)
    scores = jnp.einsum('ihd,jhd->hij', qkv_split[:, 0], qkv_split[:, 1], precision=HIGHEST) * 0.125
    scores = low_back(scores)
    allowed = (video_rows[:, None] == video_rows[None, :]) & (view_rows[None, :] == view_rows[:, None] - offset)
    scores = jnp.where(allowed[None], scores, NEG_FILL)
    weights_low = low(jax.nn.softmax(scores, axis=-1))
    mixed_heads = jnp.einsum('hij,jhd->ihd', weights_low, qkv_split[:, 2], precision=HIGHEST)
    live_rows = (view_rows >= offset).astype(jnp.float32)[:, None]
    mixed_heads = low_back(low(mixed_heads.reshape(row_count, model_width) * live_rows))
    after_attn = layer_in + low_back(matmul(mixed_heads, w_proj))
    normed_mlp = low(layer_norm(after_attn, mlp_gain))
    up_proj = low_back(matmul(normed_mlp, w_up))
    activated = low(jax.nn.gelu(up_proj, approximate=True))
    return after_attn + low_back(matmul(activated, w_down))

def whole_layer(layer_in, video_ids, view_ids, offset, params):
    block_total = layer_in.shape[0] // MB_ROWS

    def one_block(pieces):
        rows_in, video_rows, view_rows = pieces
        return block_forward(rows_in, video_rows, view_rows, offset, params)
    stacked = lax.map(jax.checkpoint(one_block), (layer_in.reshape(block_total, MB_ROWS, -1), video_ids.reshape(block_total, MB_ROWS), view_ids.reshape(block_total, MB_ROWS)))
    return stacked.reshape(layer_in.shape)

def reference(inputs, video_ids, view_ids, attn_gain, mlp_gain, w_qkv, w_proj, w_up, w_down, out_grad):
    floats = [array.astype(jnp.float32) for array in (inputs, attn_gain, mlp_gain, w_qkv, w_proj, w_up, w_down)]
    probe = jnp.zeros_like(floats[0])

    def forward(layer_zero_in, gain_attn, gain_mlp, qkv_weight, proj_weight, up_weight, down_weight, probe_in):
        first_params = (gain_attn[0], gain_mlp[0], qkv_weight[0], proj_weight[0], up_weight[0], down_weight[0])
        second_params = (gain_attn[1], gain_mlp[1], qkv_weight[1], proj_weight[1], up_weight[1], down_weight[1])
        first_out = whole_layer(layer_zero_in, video_ids, view_ids, 0, first_params)
        second_in = low_back(low(first_out) + probe_in)
        second_out = whole_layer(second_in, video_ids, view_ids, 1, second_params)
        return (first_out, second_out)
    (first_out, second_out), pullback = jax.vjp(forward, *floats, probe)
    grads = pullback((jnp.zeros_like(first_out), out_grad.astype(jnp.float32)))
    d_inputs, d_attn_gain, d_mlp_gain, d_qkv, d_proj, d_up, d_down, d_probe = grads
    layer_outputs = jnp.stack([first_out, second_out]).astype(jnp.bfloat16)
    input_grads = jnp.stack([d_inputs, d_probe]).astype(jnp.bfloat16)
    return (layer_outputs, input_grads, d_attn_gain, d_mlp_gain, d_qkv, d_proj, d_up, d_down)
```

```python
import functools

import jax
import jax.numpy as jnp
from jax import lax
from jax.experimental import pallas as pl
from jax.experimental.pallas import tpu as pltpu
from jax.sharding import PartitionSpec as P

BF = jnp.bfloat16
F32 = jnp.float32
HEAD_DIM = 64
MB_ROWS = 512
EPSILON = 1e-6
NEG_FILL = -1e30
C0 = 0.7978845608028654
C1 = 0.044715
LANES = 128
KEPT = 9
VMEM_LIMIT = 40 << 20

VM = pl.BlockSpec(memory_space=pltpu.VMEM)
ANY = pl.BlockSpec(memory_space=pl.ANY)
SM = pl.BlockSpec(memory_space=pltpu.SMEM)


def dot_nn(a, b):
    return jnp.dot(a, b, preferred_element_type=F32)


def dot_nt(a, b):
    return lax.dot_general(a, b, (((1,), (1,)), ((), ())), preferred_element_type=F32)


def normalized(x):
    center = x - jnp.mean(x, axis=-1, keepdims=True)
    inv = lax.rsqrt(jnp.mean(center * center, axis=-1, keepdims=True) + EPSILON)
    return center * inv, inv


def norm_back(d_hat, hat, inv):
    first = jnp.mean(d_hat, axis=-1, keepdims=True)
    second = jnp.mean(d_hat * hat, axis=-1, keepdims=True)
    return inv * (d_hat - first - hat * second)


def folded_rows(x):
    rows, width = x.shape
    return jnp.sum(x.reshape(rows // 8, 8, width), axis=0)


def gelu_and_slope(u):
    a = C0 * u
    b = a * (C1 * (u * u))
    gate = 0.5 + 0.5 * jnp.tanh(a + b)
    return u * gate, gate + (gate - gate * gate) * (2.0 * a + 6.0 * b)


def in_half(lane, half, inside, outside):
    return jnp.where((lane < 64) if half == 0 else (lane >= 64), inside, outside)


def forward_kernel(UNROLL, FT, threaded, active, h_ref, qa_ref, ka_ref, live_ref, g1_ref, g2_ref, *rest):
    wq, wp, wu, wd = [w.at[0] for w in rest[:4]]
    rest = rest[4 + (KEPT if threaded else 0):]
    o_ref = rest[0]
    xn_h, qkv_h, x_h, mix_h, lin_h, aft_h, nm_h, act_h, gp_h = rest[1:1 + KEPT]
    xn, qkv, pb, mix, lin, aft, nm, act, gp, osem = rest[1 + KEPT:]
    slot = active[1]
    rows, width = h_ref.shape
    hidden = wu.shape[1]
    pairs = width // LANES

    @pl.when(active[0] == 1)
    def _():
        def out(i, src, dst):
            copy = pltpu.make_async_copy(src, dst, osem.at[i])
            copy.start()
            return copy

        hat, _ = normalized(h_ref[...].astype(F32))
        xn[...] = (hat * g1_ref[...]).astype(BF)
        copies = [out(0, xn, xn_h.at[slot])]
        for t in range(3):
            cols = slice(t * width, (t + 1) * width)
            qkv[:, cols] = dot_nn(xn[...], wq[:, cols]).astype(BF)
        copies.append(out(1, qkv, qkv_h.at[slot]))
        lane = lax.broadcasted_iota(jnp.int32, (1, LANES), 1)

        @pl.loop(0, pairs // UNROLL)
        def _(step):
            pair = [step * UNROLL + u for u in range(UNROLL)]
            col = [pl.multiple_of(p * LANES, LANES) for p in pair]

            def scores(u, e):
                q = qkv[:, pl.ds(col[u], LANES)] * jnp.asarray(0.125, BF)
                k = qkv[:, pl.ds(width + col[u], LANES)]
                return dot_nt(in_half(lane, e, q, qa_ref[...]), in_half(lane, e, k, ka_ref[...]))

            def mixed(u, e, s):
                top = jnp.max(s, axis=-1, keepdims=True)
                x = jnp.exp(s - top).astype(BF)
                pb[2 * pair[u] + e] = x
                v = qkv[:, pl.ds(2 * width + col[u], LANES)]
                return dot_nn(x, in_half(lane, e, v, jnp.ones_like(v)))

            items = [(u, e) for u in range(UNROLL) for e in (0, 1)]
            s = scores(*items[0])
            parts = []
            for i, (u, e) in enumerate(items):
                following = scores(*items[i + 1]) if i + 1 < len(items) else None
                parts.append(mixed(u, e, s))
                s = following
            for u in range(UNROLL):
                a, b = parts[2 * u:2 * u + 2]
                scale = live_ref[...] / pltpu.roll(jnp.where(lane < 64, b, a), 64, 1)
                lin[:, pl.ds(col[u], LANES)] = scale
                mix[:, pl.ds(col[u], LANES)] = (jnp.where(lane < 64, a, b) * scale).astype(BF)
            heads = pl.ds(2 * UNROLL * step, 2 * UNROLL)
            pltpu.make_async_copy(pb.at[heads], x_h.at[slot, heads], osem.at[2]).start()

        copies.append(out(3, mix, mix_h.at[slot]))
        copies.append(out(4, lin, lin_h.at[slot]))
        after = h_ref[...].astype(F32) + dot_nn(mix[...], wp[...])
        aft[...] = after
        hat, _ = normalized(after)
        nm[...] = (hat * g2_ref[...]).astype(BF)
        copies.append(out(5, aft, aft_h.at[slot]))
        copies.append(out(6, nm, nm_h.at[slot]))
        tiles = hidden // FT

        def up(t):
            return dot_nn(nm[...], wu[:, t * FT:(t + 1) * FT])

        u = up(0)
        total = None
        for t in range(tiles):
            following = up(t + 1) if t + 1 < tiles else None
            value, slope = gelu_and_slope(u)
            cols = slice(t * FT, (t + 1) * FT)
            value = value.astype(BF)
            act[:, cols] = value
            gp[:, cols] = slope.astype(BF)
            pltpu.make_async_copy(act.at[:, cols], act_h.at[slot, :, cols], osem.at[7]).start()
            pltpu.make_async_copy(gp.at[:, cols], gp_h.at[slot, :, cols], osem.at[8]).start()
            term = dot_nn(value, wd[cols, :])
            total = term if total is None else total + term
            u = following
        o_ref[...] = (aft[...] + total).astype(BF)
        pltpu.make_async_copy(act, act_h.at[slot], osem.at[7]).wait()
        pltpu.make_async_copy(gp, gp_h.at[slot], osem.at[8]).wait()
        pltpu.make_async_copy(pb, x_h.at[slot], osem.at[2]).wait()
        for copy in copies:
            copy.wait()


def forward(active, h, qa, ka, live, g1, g2, weights, kept):
    rows, width = h.shape
    hidden = weights[2].shape[2]
    heads = width // HEAD_DIM
    shapes = [
        ((rows, width), BF),
        ((rows, 3 * width), BF),
        ((heads, rows, rows), BF),
        ((rows, width), BF),
        ((rows, width), F32),
        ((rows, width), F32),
        ((rows, width), BF),
        ((rows, hidden), BF),
        ((rows, hidden), BF),
    ]
    threaded = kept is not None
    outs = pl.pallas_call(
        functools.partial(forward_kernel, 2, 512, threaded),
        out_shape=[jax.ShapeDtypeStruct((rows, width), BF)]
        + [jax.ShapeDtypeStruct((2,) + s, d) for s, d in shapes],
        in_specs=[SM] + [VM] * 6 + [VM] * 4 + ([ANY] * KEPT if threaded else []),
        out_specs=[VM] + [ANY] * KEPT,
        scratch_shapes=[pltpu.VMEM(s, d) for s, d in shapes] + [pltpu.SemaphoreType.DMA((KEPT,))],
        input_output_aliases={11 + i: 1 + i for i in range(KEPT)} if threaded else {},
        compiler_params=pltpu.CompilerParams(vmem_limit_bytes=VMEM_LIMIT),
        name="forward",
    )(active, h, qa, ka, live, g1, g2, *weights, *(kept if threaded else ()))
    return outs[0], outs[1:]


def mlp_backward_kernel(FT, threaded, active, do_ref, g2_ref, wu_ref, wd_ref, gp_h, aft_h, *rest):
    rest = rest[2 if threaded else 0:]
    da_ref, gm_ref, dup_h, dpi_h, gp, aft, dup, dpi, isem, osem = rest
    slot = active[1]
    wu, wd = wu_ref.at[0], wd_ref.at[0]
    tiles = wd.shape[0] // FT

    @pl.when(active[0] == 0)
    def _():
        gm_ref[...] = jnp.zeros_like(gm_ref)

    @pl.when(active[0] == 1)
    def _():
        arrivals = []
        for t in range(tiles):
            cols = pl.ds(t * FT, FT)
            arrivals.append(pltpu.make_async_copy(gp_h.at[slot, :, cols], gp.at[:, cols], isem.at[t]))
        arrivals.append(pltpu.make_async_copy(aft_h.at[slot], aft, isem.at[tiles]))
        for copy in arrivals:
            copy.start()
        d_out = do_ref[...]

        def down(t):
            return dot_nt(d_out, wd[t * FT:(t + 1) * FT, :])

        u = down(0)
        total = None
        for t in range(tiles):
            following = down(t + 1) if t + 1 < tiles else None
            cols = slice(t * FT, (t + 1) * FT)
            arrivals[t].wait()
            value = (u * gp[:, cols].astype(F32)).astype(BF)
            dup[:, cols] = value
            pltpu.make_async_copy(dup.at[:, cols], dup_h.at[slot, :, cols], osem.at[0]).start()
            term = dot_nt(value, wu[:, cols])
            total = term if total is None else total + term
            u = following
        arrivals[tiles].wait()
        hat, inv = normalized(aft[...])
        gm_ref[...] = folded_rows(total * hat)
        d_after = d_out.astype(F32) + norm_back(total * g2_ref[...], hat, inv)
        da_ref[...] = d_after
        dpi[...] = d_after.astype(BF)
        last = pltpu.make_async_copy(dpi, dpi_h.at[slot], osem.at[1])
        last.start()
        pltpu.make_async_copy(dup, dup_h.at[slot], osem.at[0]).wait()
        last.wait()


def mlp_backward(active, d_out, g2, wu, wd, gp, aft, kept):
    rows, width = d_out.shape
    hidden = wu.shape[2]
    threaded = kept is not None
    tile = 512
    outs = pl.pallas_call(
        functools.partial(mlp_backward_kernel, tile, threaded),
        out_shape=[
            jax.ShapeDtypeStruct((rows, width), F32),
            jax.ShapeDtypeStruct((8, width), F32),
            jax.ShapeDtypeStruct((2, rows, hidden), BF),
            jax.ShapeDtypeStruct((2, rows, width), BF),
        ],
        in_specs=[SM] + [VM] * 4 + [ANY] * (4 if threaded else 2),
        out_specs=[VM, VM, ANY, ANY],
        scratch_shapes=[
            pltpu.VMEM((rows, hidden), BF),
            pltpu.VMEM((rows, width), F32),
            pltpu.VMEM((rows, hidden), BF),
            pltpu.VMEM((rows, width), BF),
            pltpu.SemaphoreType.DMA((hidden // tile + 1,)),
            pltpu.SemaphoreType.DMA((2,)),
        ],
        input_output_aliases={7: 2, 8: 3} if threaded else {},
        compiler_params=pltpu.CompilerParams(vmem_limit_bytes=VMEM_LIMIT),
        name="mlp_backward",
    )(active, d_out, g2, wu, wd, gp, aft, *(kept if threaded else ()))
    return outs[0], outs[1], outs[2:]


def attention_backward_kernel(
    UNROLL, threaded, active, da_ref, h_ref, live_ref, g1_ref, wq_ref, wp_ref, dpi_h, qkv_h, x_h, mix_h, lin_h, *rest
):
    rest = rest[1 if threaded else 0:]
    dh_ref, ga_ref, dqkv_h, dpi, qkv, x, mix, lin, dqkv, dos, qt, ot, isem, osem = rest
    slot = active[1]
    wq, wp = wq_ref.at[0], wp_ref.at[0]
    rows, width = h_ref.shape
    pairs = width // LANES

    @pl.when(active[0] == 0)
    def _():
        ga_ref[...] = jnp.zeros_like(ga_ref)

    @pl.when(active[0] == 1)
    def _():
        ins = ((dpi_h, dpi), (lin_h, lin), (mix_h, mix), (qkv_h, qkv))
        arrivals = [pltpu.make_async_copy(a.at[slot], b, isem.at[i]) for i, (a, b) in enumerate(ins)]
        for p in range(pairs):
            heads = pl.ds(2 * p, 2)
            arrivals.append(pltpu.make_async_copy(x_h.at[slot, heads], x.at[heads], isem.at[4 + p]))
        for copy in arrivals:
            copy.start()
        lane = lax.broadcasted_iota(jnp.int32, (1, LANES), 1)
        row = lax.broadcasted_iota(jnp.int32, (LANES, LANES), 0)
        column = lax.broadcasted_iota(jnp.int32, (LANES, LANES), 1)
        across = jnp.where((row < 64) != (column < 64), -1.0, 0.0).astype(BF)
        arrivals[0].wait()
        arrivals[1].wait()
        dos[...] = (dot_nt(dpi[...], wp[...]) * lin[...]).astype(BF)
        arrivals[2].wait()
        arrivals[3].wait()
        for p in range(pairs):
            cols = slice(p * LANES, (p + 1) * LANES)
            qt[cols] = qkv[:, cols].T
            ot[cols] = dos[:, cols].T

        @pl.loop(0, pairs // UNROLL)
        def _(step):
            for u in range(UNROLL):
                heads = pl.ds(0, 2)
                pltpu.make_async_copy(x_h.at[slot, heads], x.at[heads], isem.at[4 + step * UNROLL + u]).wait()
            pair = [step * UNROLL + u for u in range(UNROLL)]
            col = [pl.multiple_of(p * LANES, LANES) for p in pair]

            def row_sums(u):
                here = pl.ds(col[u], LANES)
                product = dos[:, here].astype(F32) * mix[:, here].astype(F32)
                high = product.astype(BF)
                low = (product - high.astype(F32)).astype(BF)
                negated = dot_nn(high, across) + dot_nn(low, across)
                high = negated.astype(BF)
                low = (negated - high.astype(F32)).astype(BF)
                place = lane % 64
                return jnp.where(place == 0, high, jnp.where(place == 1, low, jnp.zeros_like(high)))

            sums = [row_sums(u) for u in range(UNROLL)]

            def d_scaled(u, e):
                d_out = dos[:, pl.ds(col[u], LANES)]
                v = qkv[:, pl.ds(2 * width + col[u], LANES)]
                return dot_nt(in_half(lane, e, d_out, sums[u]), in_half(lane, e, v, jnp.ones_like(v)))

            items = [(u, e) for u in range(UNROLL) for e in (0, 1)]
            s = d_scaled(*items[0])
            results = []
            for i, (u, e) in enumerate(items):
                following = d_scaled(*items[i + 1]) if i + 1 < len(items) else None
                weights = x[2 * pair[u] + e]
                d_scores = (weights.astype(F32) * s).astype(BF)
                k = qkv[:, pl.ds(width + col[u], LANES)]
                d_query = dot_nn(d_scores, in_half(lane, e, k, jnp.zeros_like(k)))
                head = pl.ds(pl.multiple_of(col[u] + 64 * e, 64), 64)
                results.append((d_query, dot_nn(qt[head], d_scores), dot_nn(ot[head], weights)))
                s = following
            for u in range(UNROLL):
                a, b = results[2 * u:2 * u + 2]
                dqkv[:, pl.ds(col[u], LANES)] = ((a[0] + b[0]) * 0.125).astype(BF)
                d_key = jnp.concatenate([a[1], b[1]], axis=0) * 0.125
                dqkv[:, pl.ds(width + col[u], LANES)] = d_key.astype(BF).T
                d_value = jnp.concatenate([a[2], b[2]], axis=0)
                dqkv[:, pl.ds(2 * width + col[u], LANES)] = d_value.astype(BF).T

        kept = pltpu.make_async_copy(dqkv, dqkv_h.at[slot], osem.at[0])
        kept.start()
        total = None
        for t in range(3):
            cols = slice(t * width, (t + 1) * width)
            term = dot_nt(dqkv[:, cols], wq[:, cols])
            total = term if total is None else total + term
        hat, inv = normalized(h_ref[...].astype(F32))
        ga_ref[...] = folded_rows(total * hat)
        dh_ref[...] = (da_ref[...] + norm_back(total * g1_ref[...], hat, inv)).astype(BF)
        kept.wait()


def attention_backward(active, d_after, h, live, g1, wq, wp, dpi, qkv, x, mix, lin, kept):
    rows, width = h.shape
    heads = width // HEAD_DIM
    threaded = kept is not None
    return pl.pallas_call(
        functools.partial(attention_backward_kernel, 2, threaded),
        out_shape=[
            jax.ShapeDtypeStruct((rows, width), BF),
            jax.ShapeDtypeStruct((8, width), F32),
            jax.ShapeDtypeStruct((2, rows, 3 * width), BF),
        ],
        in_specs=[SM] + [VM] * 6 + [ANY] * (6 if threaded else 5),
        out_specs=[VM, VM, ANY],
        scratch_shapes=[
            pltpu.VMEM((rows, width), BF),
            pltpu.VMEM((rows, 3 * width), BF),
            pltpu.VMEM((heads, rows, rows), BF),
            pltpu.VMEM((rows, width), BF),
            pltpu.VMEM((rows, width), F32),
            pltpu.VMEM((rows, 3 * width), BF),
            pltpu.VMEM((rows, width), BF),
            pltpu.VMEM((width, rows), BF),
            pltpu.VMEM((width, rows), BF),
            pltpu.SemaphoreType.DMA((4 + width // LANES,)),
            pltpu.SemaphoreType.DMA((1,)),
        ],
        input_output_aliases={12: 2} if threaded else {},
        compiler_params=pltpu.CompilerParams(vmem_limit_bytes=VMEM_LIMIT),
        name="attention_backward",
    )(active, d_after, h, live, g1, wq, wp, dpi, qkv, x, mix, lin, *((kept,) if threaded else ()))


def mask_codes(video_rows, view_rows, offset):
    code = (video_rows - video_rows[0]) * 4 + view_rows
    place = jnp.arange(LANES) % 64
    query_code = ((code - offset)[:, None] == place[None]).astype(BF)
    key_code = jnp.where((code[:, None] == place[None]) | (place[None] >= 8), 0.0, NEG_FILL).astype(BF)
    return query_code, key_code, (view_rows >= offset).astype(F32)[:, None]


def over_tokens(left, right):
    grad = lax.dot_general(left, right, (((0, 1), (0, 1)), ((), ())), preferred_element_type=F32)
    return grad.astype(BF)


def swap(value, bit, count):
    return lax.ppermute(value, "dp", [(i, i ^ bit) for i in range(count)])


def halving_sum(grad, count):
    index = lax.axis_index("dp")
    bit = 1
    while bit < count:
        mine = (index // bit) % 2
        pieces = grad.reshape((grad.shape[0] // 2, 2) + grad.shape[1:])
        sent = lax.dynamic_index_in_dim(pieces, 1 - mine, 1, keepdims=False)
        held = lax.dynamic_index_in_dim(pieces, mine, 1, keepdims=False)
        total = held.astype(F32) + swap(sent, bit, count).astype(F32)
        bit *= 2
        grad = total if bit == count else total.astype(BF)
    return grad[0]


def on_device(inputs, video_ids, view_ids, attn_gain, mlp_gain, w_qkv, w_proj, w_up, w_down, out_grad):
    section = lax.axis_index("section")
    count = lax.axis_size("dp")
    first = section == 0
    width = inputs.shape[1]
    weights = [pltpu.with_memory_space_constraint(w, pltpu.VMEM) for w in (w_qkv, w_proj, w_up, w_down)]
    wq, wp, wu, wd = weights
    blocks = (0, 1)
    rows = [slice(b * MB_ROWS, (b + 1) * MB_ROWS) for b in blocks]
    masks = [mask_codes(video_ids[r], view_ids[r], section) for r in rows]
    on_first = [jnp.stack([1 - section, jnp.int32(b)]) for b in blocks]
    on_second = [jnp.stack([section, jnp.int32(b)]) for b in blocks]

    kept = None
    produced = []
    arrived = []
    for b in blocks:
        out, kept = forward(on_first[b], inputs[rows[b]], *masks[b], attn_gain, mlp_gain, weights, kept)
        produced.append(out)
        arrived.append(lax.ppermute(out, "section", [(0, 1)]))
    second = []
    for b in blocks:
        out, kept = forward(on_second[b], arrived[b], *masks[b], attn_gain, mlp_gain, weights, kept)
        second.append(out)
    xn, qkv, x, mix, lin, aft, nm, act, gp = kept
    layer_in = [jnp.where(first, inputs[rows[b]], arrived[b]) for b in blocks]

    mlp_kept = None
    d_qkv = None
    gain_mlp = gain_attn = 0.0
    back_second, back_first, came = [], [], []
    for stage, active in ((0, on_second), (1, on_first)):
        for b in blocks:
            d_out = out_grad[rows[b]] if stage == 0 else came[b]
            d_after, gm, mlp_kept = mlp_backward(active[b], d_out, mlp_gain, wu, wd, gp, aft, mlp_kept)
            d_in, ga, d_qkv = attention_backward(
                active[b], d_after, layer_in[b], masks[b][2], attn_gain, wq, wp, mlp_kept[1], qkv, x, mix, lin, d_qkv
            )
            gain_mlp, gain_attn = gain_mlp + gm, gain_attn + ga
            if stage == 0:
                back_second.append(d_in)
                came.append(lax.ppermute(d_in, "section", [(1, 0)]))
            else:
                back_first.append(d_in)
    d_up, d_proj_in = mlp_kept
    d_branch = jnp.stack([jnp.where(first, came[b], out_grad[rows[b]]) for b in blocks])

    def scattered(grad):
        return halving_sum(grad.reshape((count, grad.shape[0] // count) + grad.shape[1:]), count)

    g_down = scattered(over_tokens(act, d_branch))
    g_up = scattered(over_tokens(nm, d_up))
    g_proj = over_tokens(mix, d_proj_in).reshape(count, width // count, width)
    g_qkv = scattered(over_tokens(xn, d_qkv))
    gains = jnp.stack([gain_attn.sum(0), gain_mlp.sum(0)]).reshape(2, count, width // count)
    gains = jnp.pad(gains.transpose(1, 0, 2), ((0, 0), (0, 14), (0, width - width // count))).astype(BF)
    joined = halving_sum(jnp.concatenate([g_proj, gains], axis=1), count)
    share = width // count
    g_proj, gains = joined[:share], joined[share:share + 2, :share]

    layer_outputs = jnp.where(first, jnp.concatenate(produced), jnp.concatenate(second))
    input_grads = jnp.where(first, jnp.concatenate(back_first), jnp.concatenate(back_second))
    return (
        layer_outputs[None],
        input_grads[None],
        gains[0:1],
        gains[1:2],
        g_qkv[None],
        g_proj[None],
        g_up[None],
        g_down[None],
    )


def solution(mesh):
    in_specs = (
        P("dp", None),
        P("dp"),
        P("dp"),
        P("section", None),
        P("section", None),
        P("section", None, None),
        P("section", None, None),
        P("section", None, None),
        P("section", None, None),
        P("dp", None),
    )
    out_specs = (
        P("section", "dp", None),
        P("section", "dp", None),
        P("section", "dp"),
        P("section", "dp"),
        P("section", "dp", None),
        P("section", "dp", None),
        P("section", "dp", None),
        P("section", "dp", None),
    )
    return jax.shard_map(on_device, mesh=mesh, in_specs=in_specs, out_specs=out_specs, check_vma=False)
```

```python
import functools

import jax
import jax.numpy as jnp
from jax import lax
from jax.experimental import pallas as pl
from jax.experimental.pallas import tpu as pltpu
from jax.sharding import PartitionSpec as P

BF = jnp.bfloat16
F32 = jnp.float32
HEAD_DIM = 64
MB_ROWS = 512
EPSILON = 1e-6
NEG_FILL = -1e30
C0 = 0.7978845608028654
C1 = 0.044715
LANES = 128
VMEM_LIMIT = 36 << 20
HELD = 5
SHARDS = 16

VM = pl.BlockSpec(memory_space=pltpu.VMEM)
ANY = pl.BlockSpec(memory_space=pl.ANY)
MESH = pl.DeviceIdType.MESH


def dot_nn(a, b):
    return jnp.dot(a, b, preferred_element_type=F32)


def dot_nt(a, b):
    return lax.dot_general(a, b, (((1,), (1,)), ((), ())), preferred_element_type=F32)


def dot_tn(a, b):
    return lax.dot_general(a, b, (((0,), (0,)), ((), ())), preferred_element_type=F32)


def normalized(x):
    center = x - jnp.mean(x, axis=-1, keepdims=True)
    inv = lax.rsqrt(jnp.mean(center * center, axis=-1, keepdims=True) + EPSILON)
    return center * inv, inv


def norm_back(d_hat, hat, inv):
    first = jnp.mean(d_hat, axis=-1, keepdims=True)
    second = jnp.mean(d_hat * hat, axis=-1, keepdims=True)
    return inv * (d_hat - first - hat * second)


def folded_rows(x):
    rows, width = x.shape
    return jnp.sum(x.reshape(rows // 8, 8, width), axis=0)


def gelu_and_slope(u):
    a = C0 * u
    b = a * (C1 * (u * u))
    gate = 0.5 + 0.5 * jnp.tanh(a + b)
    return u * gate, gate + (gate - gate * gate) * (2.0 * a + 6.0 * b)


def in_half(lane, half, inside, outside):
    return jnp.where((lane < 64) if half == 0 else (lane >= 64), inside, outside)


def kept_shapes(rows, width, hidden):
    heads = width // HEAD_DIM
    shapes = [
        ((rows, width), BF),
        ((rows, width), BF),
        ((rows, 3 * width), BF),
        ((heads, rows, rows), BF),
        ((rows, width), BF),
        ((rows, width), F32),
        ((rows, width), F32),
        ((rows, width), BF),
        ((rows, hidden), BF),
        ((rows, width), BF),
    ]
    return shapes


def forward_kernel(UNROLL, FT, block, stage, h_h, vid_ref, view_ref, g1_ref, g2_ref, *rest):
    count = len(kept_shapes(1, HEAD_DIM, 1))
    loading = (block, stage) == (0, 0)
    sources = rest[:4]
    rest = rest[4 if loading else HELD + count:]
    wq, wp, wu, wd, gp = rest[:HELD]
    o_h = rest[HELD]
    rest = rest[1 + HELD:]
    h_k, xn_h, qkv_h, x_h, mix_h, lin_h, aft_h, nm_h, act_h, out_h = rest[:count]
    h, xn, qkv, pb, mix, lin, aft, nm, act, low = rest[count:2 * count]
    isem, wsem, osem = rest[2 * count:]
    rows, width = h.shape
    hidden = wu.shape[1]
    pairs = width // LANES
    section = lax.axis_index("section")
    loads = []
    if loading:
        loads = [pltpu.make_async_copy(a.at[0], b, wsem.at[i]) for i, (a, b) in enumerate(zip(sources, (wq, wp, wu, wd)))]
        loads[0].start()

    @pl.when(section == stage)
    def _():
        fetch = pltpu.make_async_copy(h_h if stage else h_h.at[pl.ds(block * rows, rows)], h, isem)
        fetch.start()

        def out(i, src, dst):
            copy = pltpu.make_async_copy(src, dst, osem.at[i])
            copy.start()
            return copy

        here = pl.ds(block * rows, rows)
        video = vid_ref[:, here]
        view = view_ref[:, here]
        code = (video - video[:, :1]) * 4 + view
        place = lax.broadcasted_iota(jnp.int32, (LANES, rows), 0) % 64
        query_code = jnp.where(place == code - section, 1.0, 0.0).astype(BF).T
        key_code = jnp.where((place == code) | (place >= 8), 0.0, NEG_FILL).astype(BF).T
        live = jnp.broadcast_to(jnp.where(view >= section, 1.0, 0.0), (LANES, rows)).T
        fetch.wait()
        hat, _ = normalized(h[...].astype(F32))
        xn[...] = (hat * g1_ref[...]).astype(BF)
        if loading:
            loads[0].wait()
            for copy in loads[1:]:
                copy.start()
        copies = [out(1, xn, xn_h.at[block])]
        for t in range(3):
            cols = slice(t * width, (t + 1) * width)
            qkv[:, cols] = dot_nn(xn[...], wq[:, cols]).astype(BF)
        copies.append(out(2, qkv, qkv_h.at[block]))
        tiles = hidden // FT
        copies.append(out(0, h, h_k.at[block]))
        lane = lax.broadcasted_iota(jnp.int32, (1, LANES), 1)

        @pl.loop(0, pairs // UNROLL)
        def _(step):
            pair = [step * UNROLL + u for u in range(UNROLL)]
            col = [pl.multiple_of(p * LANES, LANES) for p in pair]

            def scores(u, e):
                q = qkv[:, pl.ds(col[u], LANES)] * jnp.asarray(0.125, BF)
                k = qkv[:, pl.ds(width + col[u], LANES)]
                return dot_nt(in_half(lane, e, q, query_code), in_half(lane, e, k, key_code))

            def mixed(u, e, s):
                top = jnp.max(s, axis=-1, keepdims=True)
                x = jnp.exp(s - top).astype(BF)
                pb[2 * pair[u] + e] = x
                v = qkv[:, pl.ds(2 * width + col[u], LANES)]
                return dot_nn(x, in_half(lane, e, v, jnp.ones_like(v)))

            items = [(u, e) for u in range(UNROLL) for e in (0, 1)]
            s = scores(*items[0])
            parts = []
            for i, (u, e) in enumerate(items):
                following = scores(*items[i + 1]) if i + 1 < len(items) else None
                parts.append(mixed(u, e, s))
                s = following
            for u in range(UNROLL):
                a, b = parts[2 * u:2 * u + 2]
                scale = live / pltpu.roll(jnp.where(lane < 64, b, a), 64, 1)
                lin[:, pl.ds(col[u], LANES)] = scale
                mix[:, pl.ds(col[u], LANES)] = (jnp.where(lane < 64, a, b) * scale).astype(BF)
            heads = pl.ds(2 * UNROLL * step, 2 * UNROLL)
            pltpu.make_async_copy(pb.at[heads], x_h.at[block, heads], osem.at[3]).start()

        copies.append(out(4, mix, mix_h.at[block]))
        copies.append(out(5, lin, lin_h.at[block]))
        if loading:
            loads[1].wait()
        after = h[...].astype(F32) + dot_nn(mix[...], wp[...])
        aft[...] = after
        hat, _ = normalized(after)
        nm[...] = (hat * g2_ref[...]).astype(BF)
        copies.append(out(6, aft, aft_h.at[block]))
        copies.append(out(7, nm, nm_h.at[block]))

        def up(t):
            return dot_nn(nm[...], wu[:, t * FT:(t + 1) * FT])

        if loading:
            loads[2].wait()
            loads[3].wait()
        u = up(0)
        total = None
        for t in range(tiles):
            following = up(t + 1) if t + 1 < tiles else None
            value, slope = gelu_and_slope(u)
            cols = slice(t * FT, (t + 1) * FT)
            value = value.astype(BF)
            act[:, cols] = value
            gp[block, :, cols] = slope.astype(BF)
            pltpu.make_async_copy(act.at[:, cols], act_h.at[block, :, cols], osem.at[8]).start()
            term = dot_nn(value, wd[cols, :])
            total = term if total is None else total + term
            u = following
        result = (aft[...] + total).astype(BF)
        low[...] = result
        copies.append(out(9, low, out_h.at[block]))
        copies.append(out(10, low, o_h))
        pltpu.make_async_copy(act, act_h.at[block], osem.at[8]).wait()
        pltpu.make_async_copy(pb, x_h.at[block], osem.at[3]).wait()
        for copy in copies:
            copy.wait()

    if loading:

        @pl.when(section != stage)
        def _():
            loads[0].wait()
            for copy in loads[1:]:
                copy.start()
            for copy in loads[1:]:
                copy.wait()


def estimate(flops):
    return pl.CostEstimate(flops=flops, bytes_accessed=30 << 20, transcendentals=0)


def held_shapes(weights):
    rows, hidden = MB_ROWS, weights[2].shape[-1]
    return [pltpu.VMEM(w.shape[-2:], BF) for w in weights[:4]] + [pltpu.VMEM((2, rows, hidden), BF)]


def forward(block, stage, h, video, view, g1, g2, held, kept):
    rows, width, hidden = MB_ROWS, h.shape[1], held[2].shape[-1]
    shapes = kept_shapes(rows, width, hidden)
    n = len(shapes)
    threaded = kept is not None
    outs = pl.pallas_call(
        functools.partial(forward_kernel, 2, 512, block, stage),
        out_shape=held_shapes(held)
        + [jax.ShapeDtypeStruct((rows, width), BF)]
        + [jax.ShapeDtypeStruct((2,) + s, d) for s, d in shapes],
        in_specs=[ANY] + [VM] * 4 + ([VM] * HELD + [ANY] * n if threaded else [ANY] * 4),
        out_specs=[VM] * HELD + [ANY] * (n + 1),
        scratch_shapes=[pltpu.VMEM(s, d) for s, d in shapes]
        + [pltpu.SemaphoreType.DMA, pltpu.SemaphoreType.DMA((4,)), pltpu.SemaphoreType.DMA((n + 1,))],
        input_output_aliases={5 + i: i + (i >= HELD) for i in range(HELD + n)} if threaded else {},
        compiler_params=pltpu.CompilerParams(vmem_limit_bytes=VMEM_LIMIT),
        cost_estimate=estimate(25_000_000_000),
        name="forward",
    )(h, video, view, g1, g2, *held, *(kept if threaded else ()))
    return outs[HELD], outs[:HELD], outs[HELD + 1:]


def backward_shapes(rows, width, hidden):
    return [
        ((rows, width), BF),
        ((rows, hidden), BF),
        ((rows, width), BF),
        ((rows, 3 * width), BF),
        ((16, width), F32),
        ((rows, width), BF),
    ]


def backward_kernel(UNROLL, FT, block, stage, do_h, g1_ref, g2_ref, *rest):
    n = len(backward_shapes(1, 1, 1))
    h_k, qkv_h, x_h, mix_h, lin_h, aft_h = rest[HELD:HELD + 6]
    rest = rest[HELD + 6 + (0 if (block, stage) == (0, 1) else n):]
    wq, wp, wu, wd, gp = rest[:HELD]
    sent_h = rest[HELD]
    rest = rest[HELD + 1:]
    do_k, dup_h, dpi_h, dqkv_h, gain_h, dh_h = rest[:n]
    do, dup, dpi, dqkv, gain, low = rest[n:2 * n]
    h, qkv, x, mix, lin, aft, dos, qt, ot, da, isem, osem = rest[2 * n:]
    rows, width = h.shape
    hidden = wu.shape[1]
    pairs = width // LANES
    tiles = hidden // FT

    @pl.when(lax.axis_index("section") == stage)
    def _():
        sources = (
            (do_h.at[pl.ds(block * rows, rows)] if stage else do_h, do),
            (aft_h.at[block], aft),
            (lin_h.at[block], lin),
            (mix_h.at[block], mix),
            (qkv_h.at[block], qkv),
            (x_h.at[block], x),
            (h_k.at[block], h),
        )
        loads = [pltpu.make_async_copy(a, b, isem.at[i]) for i, (a, b) in enumerate(sources)]
        for copy in loads:
            copy.start()

        def out(i, src, dst):
            copy = pltpu.make_async_copy(src, dst, osem.at[i])
            copy.start()
            return copy

        loads[0].wait()
        d_out = do[...]

        def down(t):
            return dot_nt(d_out, wd[t * FT:(t + 1) * FT, :])

        u = down(0)
        total = None
        for t in range(tiles):
            following = down(t + 1) if t + 1 < tiles else None
            cols = slice(t * FT, (t + 1) * FT)
            value = (u * gp[block, :, cols].astype(F32)).astype(BF)
            dup[:, cols] = value
            term = dot_nt(value, wu[:, cols])
            total = term if total is None else total + term
            u = following
        copies = [out(0, do, do_k.at[block]), out(1, dup, dup_h.at[block])]
        loads[1].wait()
        hat, inv = normalized(aft[...])
        gain[8:16] = folded_rows(total * hat)
        d_after = d_out.astype(F32) + norm_back(total * g2_ref[...], hat, inv)
        da[...] = d_after
        dpi[...] = d_after.astype(BF)
        copies.append(out(2, dpi, dpi_h.at[block]))
        lane = lax.broadcasted_iota(jnp.int32, (1, LANES), 1)
        row = lax.broadcasted_iota(jnp.int32, (LANES, LANES), 0)
        column = lax.broadcasted_iota(jnp.int32, (LANES, LANES), 1)
        across = jnp.where((row < 64) != (column < 64), -1.0, 0.0).astype(BF)
        for copy in loads[2:]:
            copy.wait()
        dos[...] = (dot_nt(dpi[...], wp[...]) * lin[...]).astype(BF)
        for p in range(pairs):
            cols = slice(p * LANES, (p + 1) * LANES)
            qt[cols] = qkv[:, cols].T
            ot[cols] = dos[:, cols].T

        @pl.loop(0, pairs // UNROLL)
        def _(step):
            pair = [step * UNROLL + u for u in range(UNROLL)]
            col = [pl.multiple_of(p * LANES, LANES) for p in pair]

            def row_sums(u):
                here = pl.ds(col[u], LANES)
                product = dos[:, here].astype(F32) * mix[:, here].astype(F32)
                high = product.astype(BF)
                lower = (product - high.astype(F32)).astype(BF)
                negated = dot_nn(high, across) + dot_nn(lower, across)
                high = negated.astype(BF)
                lower = (negated - high.astype(F32)).astype(BF)
                place = lane % 64
                return jnp.where(place == 0, high, jnp.where(place == 1, lower, jnp.zeros_like(high)))

            sums = [row_sums(u) for u in range(UNROLL)]

            def d_scaled(u, e):
                d_mix = dos[:, pl.ds(col[u], LANES)]
                v = qkv[:, pl.ds(2 * width + col[u], LANES)]
                return dot_nt(in_half(lane, e, d_mix, sums[u]), in_half(lane, e, v, jnp.ones_like(v)))

            items = [(u, e) for u in range(UNROLL) for e in (0, 1)]
            s = d_scaled(*items[0])
            results = []
            for i, (u, e) in enumerate(items):
                following = d_scaled(*items[i + 1]) if i + 1 < len(items) else None
                weights = x[2 * pair[u] + e]
                d_scores = (weights.astype(F32) * s).astype(BF)
                k = qkv[:, pl.ds(width + col[u], LANES)]
                d_query = dot_nn(d_scores, in_half(lane, e, k, jnp.zeros_like(k)))
                head = pl.ds(pl.multiple_of(col[u] + 64 * e, 64), 64)
                results.append((d_query, dot_nn(qt[head], d_scores), dot_nn(ot[head], weights)))
                s = following
            for u in range(UNROLL):
                a, b = results[2 * u:2 * u + 2]
                dqkv[:, pl.ds(col[u], LANES)] = ((a[0] + b[0]) * 0.125).astype(BF)
                d_key = jnp.concatenate([a[1], b[1]], axis=0) * 0.125
                dqkv[:, pl.ds(width + col[u], LANES)] = d_key.astype(BF).T
                d_value = jnp.concatenate([a[2], b[2]], axis=0)
                dqkv[:, pl.ds(2 * width + col[u], LANES)] = d_value.astype(BF).T

        copies.append(out(3, dqkv, dqkv_h.at[block]))
        total = None
        for t in range(3):
            cols = slice(t * width, (t + 1) * width)
            term = dot_nt(dqkv[:, cols], wq[:, cols])
            total = term if total is None else total + term
        hat, inv = normalized(h[...].astype(F32))
        gain[0:8] = folded_rows(total * hat)
        copies.append(out(4, gain, gain_h.at[block]))
        result = (da[...] + norm_back(total * g1_ref[...], hat, inv)).astype(BF)
        low[...] = result
        copies.append(out(5, low, dh_h.at[block]))
        copies.append(out(6, low, sent_h))
        for copy in copies:
            copy.wait()


def backward(block, stage, d_out, g1, g2, held, saved, kept):
    rows, width, hidden = MB_ROWS, d_out.shape[1], held[2].shape[-1]
    shapes = backward_shapes(rows, width, hidden)
    n = len(shapes)
    threaded = kept is not None
    h, xn, qkv, x, mix, lin, aft, nm, act, produced = saved
    ins = (h, qkv, x, mix, lin, aft)
    aliases = {3 + i: i for i in range(HELD)}
    if threaded:
        aliases.update({3 + HELD + len(ins) + i: HELD + 1 + i for i in range(n)})
    outs = pl.pallas_call(
        functools.partial(backward_kernel, 2, 512, block, stage),
        out_shape=held_shapes(held)
        + [jax.ShapeDtypeStruct((rows, width), BF)]
        + [jax.ShapeDtypeStruct((2,) + s, d) for s, d in shapes],
        in_specs=[ANY] + [VM] * (2 + HELD) + [ANY] * (len(ins) + (n if threaded else 0)),
        out_specs=[VM] * HELD + [ANY] * (n + 1),
        scratch_shapes=[pltpu.VMEM(s, d) for s, d in shapes]
        + [pltpu.VMEM(a.shape[1:], a.dtype) for a in ins]
        + [pltpu.VMEM((rows, width), BF), pltpu.VMEM((width, rows), BF), pltpu.VMEM((width, rows), BF)]
        + [pltpu.VMEM((rows, width), F32)]
        + [pltpu.SemaphoreType.DMA((len(ins) + 1,)), pltpu.SemaphoreType.DMA((n + 1,))],
        input_output_aliases=aliases,
        compiler_params=pltpu.CompilerParams(vmem_limit_bytes=VMEM_LIMIT),
        cost_estimate=estimate(28_000_000_000),
        name="backward",
    )(d_out, g1, g2, *held, *ins, *(kept if threaded else ()))
    return outs[HELD], outs[:HELD], outs[HELD + 1:]


def shard_place(shard, z_first):
    x, near, far = (shard >> 1) & 1, (shard >> 2) & 1, (shard >> 3) & 1
    return 4 * near + 2 * far + x if z_first else 4 * x + 2 * near + far


def part_rows(width):
    share = width // SHARDS
    return [share] * 3 + [share + 16] + [share] * 8


def z_first_parts():
    return (2, 7)


def weight_grad_kernel(left_h, right_h, gain_ref, g_h, a, b, o, gain, isem, osem, gsem):
    tokens, width = a.shape[1] * a.shape[2], a.shape[3]
    share = width // SHARDS
    mine = lax.rem(lax.axis_index("dp"), 2)
    units = len(right_h)

    def loads(k, slot):
        left, lane_a = left_h[k]
        right, lane_b = right_h[k]
        return (
            pltpu.make_async_copy(left.at[:, :, pl.ds(lane_a * width, width)], a.at[slot], isem.at[slot]),
            pltpu.make_async_copy(right.at[:, :, pl.ds(lane_b * width, width)], b.at[slot], isem.at[2 + slot]),
        )

    def stores(k, slot):
        copies = []
        if k < 8:
            base = share * k + (16 if k >= 4 else 0)
            for d in range(SHARDS):
                side = lax.rem(mine + d % 2, 2)
                place = shard_place(d, k in z_first_parts())
                copies.append((pl.ds(d * share, share), side, place, pl.ds(base, share)))
        else:
            for i in range(4):
                d = 4 * (k - 8) + i
                side = lax.rem(mine + d % 2, 2)
                base = 8 * share + 16
                copies.append((pl.ds(i * 4 * share, 4 * share), side, shard_place(d, False), pl.ds(base, 4 * share)))
        return [
            pltpu.make_async_copy(o.at[slot, src], g_h.at[side, place, dst], osem.at[slot])
            for src, side, place, dst in copies
        ]

    for copy in loads(0, 0):
        copy.start()
    row = lax.broadcasted_iota(jnp.int32, (16, width), 0)
    both = gain_ref[0] + gain_ref[1]
    first = jnp.sum(both[0:8], axis=0, keepdims=True)
    second = jnp.sum(both[8:16], axis=0, keepdims=True)
    gain[...] = jnp.where(row == 0, first, jnp.where(row == 1, second, 0.0)).astype(BF)
    for side in range(2):
        for place in range(SHARDS // 2):
            pltpu.make_async_copy(gain, g_h.at[side, place, pl.ds(4 * share, 16)], gsem).start()

    @pl.loop(0, units)
    def _(k):
        slot = lax.rem(k, 2)
        for j in range(units):

            @pl.when(k + 1 == j)
            def _():
                for copy in loads(j, j % 2):
                    copy.start()

        for copy in loads(0, slot):
            copy.wait()

        @pl.when(k >= 2)
        def _():
            pltpu.make_async_copy(o.at[slot], o.at[slot], osem.at[slot]).wait()

        left = a[slot].reshape(tokens, width)
        right = b[slot].reshape(tokens, width)
        o[slot] = dot_tn(left, right).astype(BF)
        for j in range(units):

            @pl.when(k == j)
            def _():
                for copy in stores(j, j % 2):
                    copy.start()

    for slot in range(2):
        pltpu.make_async_copy(o.at[slot], o.at[slot], osem.at[slot]).wait()
    for side in range(2):
        for place in range(SHARDS // 2):
            pltpu.make_async_copy(gain, g_h.at[side, place, pl.ds(4 * share, 16)], gsem).wait()


def weight_grads(pairs, gains):
    rows, width = pairs[0][0].shape[1:]
    arrays, units = [], []
    for left, right, count, split in pairs:
        for j in range(count):
            units.append((len(arrays), j if split == 0 else 0, len(arrays) + 1, j if split == 1 else 0))
        arrays += [left, right]
    n = len(arrays)

    def kernel(*refs):
        ins, rest = refs[:n], refs[n:]
        left = [(ins[u[0]], u[1]) for u in units]
        right = [(ins[u[2]], u[3]) for u in units]
        weight_grad_kernel(left, right, *rest)

    return pl.pallas_call(
        kernel,
        out_shape=jax.ShapeDtypeStruct((2, SHARDS // 2, sum(part_rows(width)) , width), BF),
        in_specs=[ANY] * n + [VM],
        out_specs=ANY,
        scratch_shapes=[
            pltpu.VMEM((2, 2, rows, width), BF),
            pltpu.VMEM((2, 2, rows, width), BF),
            pltpu.VMEM((2, width, width), BF),
            pltpu.VMEM((16, width), BF),
            pltpu.SemaphoreType.DMA((4,)),
            pltpu.SemaphoreType.DMA((2,)),
            pltpu.SemaphoreType.DMA,
        ],
        compiler_params=pltpu.CompilerParams(vmem_limit_bytes=VMEM_LIMIT),
        cost_estimate=estimate(20_000_000_000),
        name="weight_grads",
    )(*arrays, gains)


def reduce_kernel(g_h, q_ref, p_ref, n_ref, u_ref, d_ref, acc, got0, got1, got2, got3, lsem, ssem, rsem):
    width = p_ref.shape[1]
    share = width // SHARDS
    sizes = part_rows(width)
    parts = len(sizes)
    starts = [sum(sizes[:i]) for i in range(parts)]
    index = lax.axis_index("dp")
    bits = [lax.rem(index // (1 << k), 2) for k in range(4)]

    def partner(k):
        return {"dp": index + (1 << k) * (1 - 2 * bits[k])}

    barrier = pltpu.get_barrier_semaphore()
    for k in range(4):
        pl.semaphore_signal(barrier, inc=1, device_id=partner(k), device_id_type=MESH)
    pl.semaphore_wait(barrier, 4)
    got = (got0, got1, got2, got3)

    def order(t):
        return (0, 2, 3, 1) if t in z_first_parts() else (0, 1, 2, 3)

    def held(t, stage):
        base = 0
        for level in range(1, stage + 1):
            base = base + (8 >> level) * bits[order(t)[level]]
        return base

    def send(t, stage):
        rows = pl.ds(starts[t], sizes[t])
        k = order(t)[stage]
        if stage == 0:
            source = g_h.at[1, :, rows]
        else:
            half = 8 >> stage
            source = acc.at[pl.ds(held(t, stage - 1) + half * (1 - bits[k]), half), rows]
        return pltpu.make_async_remote_copy(
            src_ref=source,
            dst_ref=got[stage].at[:, rows],
            send_sem=ssem.at[stage, t],
            recv_sem=rsem.at[stage, t],
            device_id=partner(k),
            device_id_type=MESH,
        )

    def local(t):
        rows = pl.ds(starts[t], sizes[t])
        return pltpu.make_async_copy(g_h.at[0, :, rows], acc.at[:, rows], lsem.at[t])

    def begin(t):
        send(t, 0).start()
        local(t).start()

    def combine(t, stage):
        rows = pl.ds(starts[t], sizes[t])
        base = held(t, stage)
        send(t, stage).wait_recv()

        @pl.loop(0, 8 >> stage)
        def _(i):
            total = acc[base + i, rows].astype(F32) + got[stage][i, rows].astype(F32)
            acc[base + i, rows] = total.astype(BF)

        send(t, stage + 1).start()

    def finish(t):
        rows = pl.ds(starts[t], sizes[t])
        send(t, 3).wait_recv()
        total = acc[held(t, 3), rows].astype(F32) + got3[0, rows].astype(F32)
        if t < 3:
            q_ref[:, t * width:(t + 1) * width] = total
        elif t == 3:
            p_ref[...] = total[:share]
            n_ref[...] = total[share:]
        elif t < 8:
            u_ref[:, (t - 4) * width:(t - 3) * width] = total
        else:
            d_ref[(t - 8) * share:(t - 7) * share] = total

    ahead = 3
    for t in range(ahead):
        begin(t)
    for t in range(parts + 3):
        if t < parts:
            local(t).wait()
            combine(t, 0)
            if t + ahead < parts:
                begin(t + ahead)
        if 0 <= t - 1 < parts:
            combine(t - 1, 1)
        if 0 <= t - 2 < parts:
            combine(t - 2, 2)
        if 0 <= t - 3 < parts:
            finish(t - 3)
    for t in range(parts):
        for stage in range(4):
            send(t, stage).wait_send()


def reduce_shards(packed, hidden):
    rows, width = packed.shape[2:]
    share = width // SHARDS
    parts = len(part_rows(width))
    return pl.pallas_call(
        reduce_kernel,
        out_shape=[
            jax.ShapeDtypeStruct((share, 3 * width), F32),
            jax.ShapeDtypeStruct((share, width), F32),
            jax.ShapeDtypeStruct((16, width), F32),
            jax.ShapeDtypeStruct((share, hidden), F32),
            jax.ShapeDtypeStruct((hidden // SHARDS, width), F32),
        ],
        in_specs=[ANY],
        out_specs=[VM] * 5,
        scratch_shapes=[
            pltpu.VMEM((8, rows, width), BF),
            pltpu.VMEM((8, rows, width), BF),
            pltpu.VMEM((4, rows, width), BF),
            pltpu.VMEM((2, rows, width), BF),
            pltpu.VMEM((1, rows, width), BF),
            pltpu.SemaphoreType.DMA((parts,)),
            pltpu.SemaphoreType.DMA((4, parts)),
            pltpu.SemaphoreType.DMA((4, parts)),
        ],
        compiler_params=pltpu.CompilerParams(
            vmem_limit_bytes=VMEM_LIMIT, collective_id=0, has_side_effects=True
        ),
        name="reduce_shards",
    )(packed)


def over_tokens(left, right):
    grad = lax.dot_general(left, right, (((0, 1), (0, 1)), ((), ())), preferred_element_type=F32)
    return grad.astype(BF)


def swap(value, bit, count):
    return lax.ppermute(value, "dp", [(i, i ^ bit) for i in range(count)])


def halving_sum(grad, count):
    index = lax.axis_index("dp")
    bit = 1
    while bit < count:
        mine = (index // bit) % 2
        pieces = grad.reshape((grad.shape[0] // 2, 2) + grad.shape[1:])
        sent = lax.dynamic_index_in_dim(pieces, 1 - mine, 1, keepdims=False)
        held = lax.dynamic_index_in_dim(pieces, mine, 1, keepdims=False)
        total = held.astype(F32) + swap(sent, bit, count).astype(F32)
        bit *= 2
        grad = total if bit == count else total.astype(BF)
    return grad[0]


def scattered(grad, count):
    return halving_sum(grad.reshape((count, grad.shape[0] // count) + grad.shape[1:]), count)


def on_device(inputs, video_ids, view_ids, attn_gain, mlp_gain, w_qkv, w_proj, w_up, w_down, out_grad):
    count = lax.axis_size("dp")
    rows, width = inputs.shape
    held = (w_qkv, w_proj, w_up, w_down)
    video, view = video_ids.reshape(1, rows), view_ids.reshape(1, rows)
    gains = (attn_gain, mlp_gain)

    saved = None
    arrived = []
    for block in (0, 1):
        out, held, saved = forward(block, 0, inputs, video, view, *gains, held, saved)
        arrived.append(lax.ppermute(out, "section", [(0, 1)]))
    for block in (0, 1):
        _, held, saved = forward(block, 1, arrived[block], video, view, *gains, held, saved)
    kept = None
    came = []
    for block in (0, 1):
        d_in, held, kept = backward(block, 1, out_grad, *gains, held, saved, kept)
        came.append(lax.ppermute(d_in, "section", [(1, 0)]))
    for block in (0, 1):
        _, held, kept = backward(block, 0, came[block], *gains, held, saved, kept)
    h, xn, qkv, x, mix, lin, aft, nm, act, layer_outputs = saved
    d_branch, d_up, d_proj_in, d_qkv, gain_grads, input_grads = kept

    hidden = w_up.shape[2]
    share = width // count
    if count == SHARDS and hidden == 4 * width:
        packed = weight_grads(
            ((xn, d_qkv, 3, 1), (mix, d_proj_in, 1, 1), (nm, d_up, 4, 1), (act, d_branch, 4, 0)), gain_grads
        )
        g_qkv, g_proj, gain_rows, g_up, g_down = reduce_shards(packed, hidden)
        here = lax.axis_index("dp") * share
        gain_sums = lax.dynamic_slice(gain_rows, (0, here), (2, share))
    else:
        g_down = scattered(over_tokens(act, d_branch), count)
        g_up = scattered(over_tokens(nm, d_up), count)
        g_proj = over_tokens(mix, d_proj_in).reshape(count, share, width)
        g_qkv = scattered(over_tokens(xn, d_qkv), count)
        gain_sums = gain_grads.reshape(2, 2, 8, width).sum((0, 2)).reshape(2, count, share)
        gain_sums = jnp.pad(gain_sums.transpose(1, 0, 2), ((0, 0), (0, 14), (0, width - share))).astype(BF)
        joined = halving_sum(jnp.concatenate([g_proj, gain_sums], axis=1), count)
        g_proj, gain_sums = joined[:share], joined[share:share + 2, :share]
    return (
        layer_outputs.reshape(1, rows, width),
        input_grads.reshape(1, rows, width),
        gain_sums[0:1],
        gain_sums[1:2],
        g_qkv[None],
        g_proj[None],
        g_up[None],
        g_down[None],
    )


def solution(mesh):
    in_specs = (
        P("dp", None),
        P("dp"),
        P("dp"),
        P("section", None),
        P("section", None),
        P("section", None, None),
        P("section", None, None),
        P("section", None, None),
        P("section", None, None),
        P("dp", None),
    )
    out_specs = (
        P("section", "dp", None),
        P("section", "dp", None),
        P("section", "dp"),
        P("section", "dp"),
        P("section", "dp", None),
        P("section", "dp", None),
        P("section", "dp", None),
        P("section", "dp", None),
    )
    return jax.shard_map(on_device, mesh=mesh, in_specs=in_specs, out_specs=out_specs, check_vma=False)
```

```python
import functools

import jax
import jax.numpy as jnp
from jax import lax
from jax.experimental import pallas as pl
from jax.experimental.pallas import tpu as pltpu
from jax.sharding import PartitionSpec as P

BF = jnp.bfloat16
F32 = jnp.float32
HEAD_DIM = 64
MB_ROWS = 512
EPSILON = 1e-6
NEG_FILL = -1e30
C0 = 0.7978845608028654
C1 = 0.044715
LANES = 128
VMEM_LIMIT = 43 << 20
HELD = 5
SHARDS = 16
LAG = 2

VM = pl.BlockSpec(memory_space=pltpu.VMEM)
ANY = pl.BlockSpec(memory_space=pl.ANY)
MESH = pl.DeviceIdType.MESH


def dot_nn(a, b):
    return jnp.dot(a, b, preferred_element_type=F32)


def dot_nt(a, b):
    return lax.dot_general(a, b, (((1,), (1,)), ((), ())), preferred_element_type=F32)


def dot_tn(a, b):
    return lax.dot_general(a, b, (((0,), (0,)), ((), ())), preferred_element_type=F32)


def normalized(x):
    center = x - jnp.mean(x, axis=-1, keepdims=True)
    inv = lax.rsqrt(jnp.mean(center * center, axis=-1, keepdims=True) + EPSILON)
    return center * inv, inv


def norm_back(d_hat, hat, inv):
    first = jnp.mean(d_hat, axis=-1, keepdims=True)
    second = jnp.mean(d_hat * hat, axis=-1, keepdims=True)
    return inv * (d_hat - first - hat * second)


def folded_rows(x):
    rows, width = x.shape
    return jnp.sum(x.reshape(rows // 8, 8, width), axis=0)


def gelu_and_slope(u):
    a = C0 * u
    b = a * (C1 * (u * u))
    gate = 0.5 + 0.5 * jnp.tanh(a + b)
    return u * gate, gate + (gate - gate * gate) * (2.0 * a + 6.0 * b)


def in_half(lane, half, inside, outside):
    return jnp.where((lane < 64) if half == 0 else (lane >= 64), inside, outside)


def kept_shapes(rows, width, hidden):
    heads = width // HEAD_DIM
    shapes = [
        ((rows, width), BF),
        ((rows, width), BF),
        ((rows, 3 * width), BF),
        ((heads, rows, rows), BF),
        ((rows, width), BF),
        ((rows, width), F32),
        ((rows, width), F32),
        ((rows, width), BF),
        ((rows, hidden), BF),
        ((rows, width), BF),
    ]
    return shapes


def forward_kernel(UNROLL, FT, block, stage, h_h, vid_ref, view_ref, g1_ref, g2_ref, *rest):
    count = len(kept_shapes(1, HEAD_DIM, 1))
    loading = (block, stage) == (0, 0)
    sources = rest[:4]
    rest = rest[4 if loading else HELD + count:]
    wq, wp, wu, wd, gp = rest[:HELD]
    o_h = rest[HELD]
    rest = rest[1 + HELD:]
    h_k, xn_h, qkv_h, x_h, mix_h, lin_h, aft_h, nm_h, act_h, out_h = rest[:count]
    h, xn, qkv, pb, mix, lin, aft, nm, act, low = rest[count:2 * count]
    isem, wsem, osem = rest[2 * count:]
    rows, width = h.shape
    hidden = wu.shape[1]
    pairs = width // LANES
    section = lax.axis_index("section")
    loads = []
    if loading:
        loads = [pltpu.make_async_copy(a.at[0], b, wsem.at[i]) for i, (a, b) in enumerate(zip(sources, (wq, wp, wu, wd)))]
        loads[0].start()

    @pl.when(section == stage)
    def _():
        fetch = pltpu.make_async_copy(h_h if stage else h_h.at[pl.ds(block * rows, rows)], h, isem)
        fetch.start()

        def out(i, src, dst):
            copy = pltpu.make_async_copy(src, dst, osem.at[i])
            copy.start()
            return copy

        here = pl.ds(block * rows, rows)
        video = vid_ref[:, here]
        view = view_ref[:, here]
        code = (video - video[:, :1]) * 4 + view
        place = lax.broadcasted_iota(jnp.int32, (LANES, rows), 0) % 64
        query_code = jnp.where(place == code - section, 1.0, 0.0).astype(BF).T
        key_code = jnp.where((place == code) | (place >= 8), 0.0, NEG_FILL).astype(BF).T
        live = jnp.broadcast_to(jnp.where(view >= section, 1.0, 0.0), (LANES, rows)).T
        fetch.wait()
        hat, _ = normalized(h[...].astype(F32))
        xn[...] = (hat * g1_ref[...]).astype(BF)
        if loading:
            loads[0].wait()
            for copy in loads[1:]:
                copy.start()
        copies = [out(1, xn, xn_h.at[block])]
        for t in range(3):
            cols = slice(t * width, (t + 1) * width)
            qkv[:, cols] = dot_nn(xn[...], wq[:, cols]).astype(BF)
        copies.append(out(2, qkv, qkv_h.at[block]))
        tiles = hidden // FT
        copies.append(out(0, h, h_k.at[block]))
        lane = lax.broadcasted_iota(jnp.int32, (1, LANES), 1)

        @pl.loop(0, pairs // UNROLL)
        def _(step):
            pair = [step * UNROLL + u for u in range(UNROLL)]
            col = [pl.multiple_of(p * LANES, LANES) for p in pair]

            def scores(u, e):
                q = qkv[:, pl.ds(col[u], LANES)] * jnp.asarray(0.125, BF)
                k = qkv[:, pl.ds(width + col[u], LANES)]
                return dot_nt(in_half(lane, e, q, query_code), in_half(lane, e, k, key_code))

            def mixed(u, e, s):
                top = jnp.max(s, axis=-1, keepdims=True)
                x = jnp.exp(s - top).astype(BF)
                pb[2 * pair[u] + e] = x
                v = qkv[:, pl.ds(2 * width + col[u], LANES)]
                return dot_nn(x, in_half(lane, e, v, jnp.ones_like(v)))

            items = [(u, e) for u in range(UNROLL) for e in (0, 1)]
            s = scores(*items[0])
            parts = []
            for i, (u, e) in enumerate(items):
                following = scores(*items[i + 1]) if i + 1 < len(items) else None
                parts.append(mixed(u, e, s))
                s = following
            for u in range(UNROLL):
                a, b = parts[2 * u:2 * u + 2]
                scale = live / pltpu.roll(jnp.where(lane < 64, b, a), 64, 1)
                lin[:, pl.ds(col[u], LANES)] = scale
                mix[:, pl.ds(col[u], LANES)] = (jnp.where(lane < 64, a, b) * scale).astype(BF)
            heads = pl.ds(2 * UNROLL * step, 2 * UNROLL)
            pltpu.make_async_copy(pb.at[heads], x_h.at[block, heads], osem.at[3]).start()

        copies.append(out(4, mix, mix_h.at[block]))
        copies.append(out(5, lin, lin_h.at[block]))
        if loading:
            loads[1].wait()
        after = h[...].astype(F32) + dot_nn(mix[...], wp[...])
        aft[...] = after
        hat, _ = normalized(after)
        nm[...] = (hat * g2_ref[...]).astype(BF)
        copies.append(out(6, aft, aft_h.at[block]))
        copies.append(out(7, nm, nm_h.at[block]))

        def up(t):
            return dot_nn(nm[...], wu[:, t * FT:(t + 1) * FT])

        if loading:
            loads[2].wait()
            loads[3].wait()
        u = up(0)
        total = None
        for t in range(tiles):
            following = up(t + 1) if t + 1 < tiles else None
            value, slope = gelu_and_slope(u)
            cols = slice(t * FT, (t + 1) * FT)
            value = value.astype(BF)
            act[:, cols] = value
            gp[block, :, cols] = slope.astype(BF)
            pltpu.make_async_copy(act.at[:, cols], act_h.at[block, :, cols], osem.at[8]).start()
            term = dot_nn(value, wd[cols, :])
            total = term if total is None else total + term
            u = following
        result = (aft[...] + total).astype(BF)
        low[...] = result
        copies.append(out(9, low, out_h.at[block]))
        copies.append(out(10, low, o_h))
        pltpu.make_async_copy(act, act_h.at[block], osem.at[8]).wait()
        pltpu.make_async_copy(pb, x_h.at[block], osem.at[3]).wait()
        for copy in copies:
            copy.wait()

    if loading:

        @pl.when(section != stage)
        def _():
            loads[0].wait()
            for copy in loads[1:]:
                copy.start()
            for copy in loads[1:]:
                copy.wait()


def estimate(flops):
    return pl.CostEstimate(flops=flops, bytes_accessed=30 << 20, transcendentals=0)


def held_shapes(weights):
    rows, hidden = MB_ROWS, weights[2].shape[-1]
    return [pltpu.VMEM(w.shape[-2:], BF) for w in weights[:4]] + [pltpu.VMEM((2, rows, hidden), BF)]


def forward(block, stage, h, video, view, g1, g2, held, kept):
    rows, width, hidden = MB_ROWS, h.shape[1], held[2].shape[-1]
    shapes = kept_shapes(rows, width, hidden)
    n = len(shapes)
    threaded = kept is not None
    outs = pl.pallas_call(
        functools.partial(forward_kernel, 2, 512, block, stage),
        out_shape=held_shapes(held)
        + [jax.ShapeDtypeStruct((rows, width), BF)]
        + [jax.ShapeDtypeStruct((2,) + s, d) for s, d in shapes],
        in_specs=[ANY] + [VM] * 4 + ([VM] * HELD + [ANY] * n if threaded else [ANY] * 4),
        out_specs=[VM] * HELD + [ANY] * (n + 1),
        scratch_shapes=[pltpu.VMEM(s, d) for s, d in shapes]
        + [pltpu.SemaphoreType.DMA, pltpu.SemaphoreType.DMA((4,)), pltpu.SemaphoreType.DMA((n + 1,))],
        input_output_aliases={5 + i: i + (i >= HELD) for i in range(HELD + n)} if threaded else {},
        compiler_params=pltpu.CompilerParams(vmem_limit_bytes=VMEM_LIMIT),
        cost_estimate=estimate(25_000_000_000),
        name="forward",
    )(h, video, view, g1, g2, *held, *(kept if threaded else ()))
    return outs[HELD], outs[:HELD], outs[HELD + 1:]


def backward_shapes(rows, width, hidden):
    return [
        ((rows, width), BF),
        ((rows, hidden), BF),
        ((rows, width), BF),
        ((rows, 3 * width), BF),
        ((16, width), F32),
        ((rows, width), BF),
    ]


def backward_kernel(UNROLL, FT, block, stage, do_h, g1_ref, g2_ref, *rest):
    n = len(backward_shapes(1, 1, 1))
    h_k, qkv_h, x_h, mix_h, lin_h, aft_h = rest[HELD:HELD + 6]
    rest = rest[HELD + 6 + (0 if (block, stage) == (0, 1) else n):]
    wq, wp, wu, wd, gp = rest[:HELD]
    sent_h = rest[HELD]
    rest = rest[HELD + 1:]
    do_k, dup_h, dpi_h, dqkv_h, gain_h, dh_h = rest[:n]
    do, dup, dpi, dqkv, gain, low = rest[n:2 * n]
    h, qkv, x, mix, lin, aft, dos, qt, ot, da, isem, osem = rest[2 * n:]
    rows, width = h.shape
    hidden = wu.shape[1]
    pairs = width // LANES
    tiles = hidden // FT

    @pl.when(lax.axis_index("section") == stage)
    def _():
        sources = (
            (do_h.at[pl.ds(block * rows, rows)] if stage else do_h, do),
            (aft_h.at[block], aft),
            (lin_h.at[block], lin),
            (mix_h.at[block], mix),
            (qkv_h.at[block], qkv),
            (x_h.at[block], x),
            (h_k.at[block], h),
        )
        loads = [pltpu.make_async_copy(a, b, isem.at[i]) for i, (a, b) in enumerate(sources)]
        for copy in loads:
            copy.start()

        def out(i, src, dst):
            copy = pltpu.make_async_copy(src, dst, osem.at[i])
            copy.start()
            return copy

        loads[0].wait()
        d_out = do[...]

        def down(t):
            return dot_nt(d_out, wd[t * FT:(t + 1) * FT, :])

        u = down(0)
        total = None
        for t in range(tiles):
            following = down(t + 1) if t + 1 < tiles else None
            cols = slice(t * FT, (t + 1) * FT)
            value = (u * gp[block, :, cols].astype(F32)).astype(BF)
            dup[:, cols] = value
            term = dot_nt(value, wu[:, cols])
            total = term if total is None else total + term
            u = following
        copies = [out(0, do, do_k.at[block]), out(1, dup, dup_h.at[block])]
        loads[1].wait()
        hat, inv = normalized(aft[...])
        gain[8:16] = folded_rows(total * hat)
        d_after = d_out.astype(F32) + norm_back(total * g2_ref[...], hat, inv)
        da[...] = d_after
        dpi[...] = d_after.astype(BF)
        copies.append(out(2, dpi, dpi_h.at[block]))
        lane = lax.broadcasted_iota(jnp.int32, (1, LANES), 1)
        row = lax.broadcasted_iota(jnp.int32, (LANES, LANES), 0)
        column = lax.broadcasted_iota(jnp.int32, (LANES, LANES), 1)
        across = jnp.where((row < 64) != (column < 64), -1.0, 0.0).astype(BF)
        for copy in loads[2:]:
            copy.wait()
        dos[...] = (dot_nt(dpi[...], wp[...]) * lin[...]).astype(BF)
        for p in range(pairs):
            cols = slice(p * LANES, (p + 1) * LANES)
            qt[cols] = qkv[:, cols].T
            ot[cols] = dos[:, cols].T

        @pl.loop(0, pairs // UNROLL)
        def _(step):
            pair = [step * UNROLL + u for u in range(UNROLL)]
            col = [pl.multiple_of(p * LANES, LANES) for p in pair]

            def row_sums(u):
                here = pl.ds(col[u], LANES)
                product = dos[:, here].astype(F32) * mix[:, here].astype(F32)
                high = product.astype(BF)
                lower = (product - high.astype(F32)).astype(BF)
                negated = dot_nn(high, across) + dot_nn(lower, across)
                high = negated.astype(BF)
                lower = (negated - high.astype(F32)).astype(BF)
                place = lane % 64
                return jnp.where(place == 0, high, jnp.where(place == 1, lower, jnp.zeros_like(high)))

            sums = [row_sums(u) for u in range(UNROLL)]

            def d_scaled(u, e):
                d_mix = dos[:, pl.ds(col[u], LANES)]
                v = qkv[:, pl.ds(2 * width + col[u], LANES)]
                return dot_nt(in_half(lane, e, d_mix, sums[u]), in_half(lane, e, v, jnp.ones_like(v)))

            items = [(u, e) for u in range(UNROLL) for e in (0, 1)]
            s = d_scaled(*items[0])
            results = []
            for i, (u, e) in enumerate(items):
                following = d_scaled(*items[i + 1]) if i + 1 < len(items) else None
                weights = x[2 * pair[u] + e]
                d_scores = (weights.astype(F32) * s).astype(BF)
                k = qkv[:, pl.ds(width + col[u], LANES)]
                d_query = dot_nn(d_scores, in_half(lane, e, k, jnp.zeros_like(k)))
                head = pl.ds(pl.multiple_of(col[u] + 64 * e, 64), 64)
                results.append((d_query, dot_nn(qt[head], d_scores), dot_nn(ot[head], weights)))
                s = following
            for u in range(UNROLL):
                a, b = results[2 * u:2 * u + 2]
                dqkv[:, pl.ds(col[u], LANES)] = ((a[0] + b[0]) * 0.125).astype(BF)
                d_key = jnp.concatenate([a[1], b[1]], axis=0) * 0.125
                dqkv[:, pl.ds(width + col[u], LANES)] = d_key.astype(BF).T
                d_value = jnp.concatenate([a[2], b[2]], axis=0)
                dqkv[:, pl.ds(2 * width + col[u], LANES)] = d_value.astype(BF).T

        copies.append(out(3, dqkv, dqkv_h.at[block]))
        total = None
        for t in range(3):
            cols = slice(t * width, (t + 1) * width)
            term = dot_nt(dqkv[:, cols], wq[:, cols])
            total = term if total is None else total + term
        hat, inv = normalized(h[...].astype(F32))
        gain[0:8] = folded_rows(total * hat)
        copies.append(out(4, gain, gain_h.at[block]))
        result = (da[...] + norm_back(total * g1_ref[...], hat, inv)).astype(BF)
        low[...] = result
        copies.append(out(5, low, dh_h.at[block]))
        copies.append(out(6, low, sent_h))
        for copy in copies:
            copy.wait()


def backward(block, stage, d_out, g1, g2, held, saved, kept):
    rows, width, hidden = MB_ROWS, d_out.shape[1], held[2].shape[-1]
    shapes = backward_shapes(rows, width, hidden)
    n = len(shapes)
    threaded = kept is not None
    h, xn, qkv, x, mix, lin, aft, nm, act, produced = saved
    ins = (h, qkv, x, mix, lin, aft)
    aliases = {3 + i: i for i in range(HELD)}
    if threaded:
        aliases.update({3 + HELD + len(ins) + i: HELD + 1 + i for i in range(n)})
    outs = pl.pallas_call(
        functools.partial(backward_kernel, 2, 512, block, stage),
        out_shape=held_shapes(held)
        + [jax.ShapeDtypeStruct((rows, width), BF)]
        + [jax.ShapeDtypeStruct((2,) + s, d) for s, d in shapes],
        in_specs=[ANY] + [VM] * (2 + HELD) + [ANY] * (len(ins) + (n if threaded else 0)),
        out_specs=[VM] * HELD + [ANY] * (n + 1),
        scratch_shapes=[pltpu.VMEM(s, d) for s, d in shapes]
        + [pltpu.VMEM(a.shape[1:], a.dtype) for a in ins]
        + [pltpu.VMEM((rows, width), BF), pltpu.VMEM((width, rows), BF), pltpu.VMEM((width, rows), BF)]
        + [pltpu.VMEM((rows, width), F32)]
        + [pltpu.SemaphoreType.DMA((len(ins) + 1,)), pltpu.SemaphoreType.DMA((n + 1,))],
        input_output_aliases=aliases,
        compiler_params=pltpu.CompilerParams(vmem_limit_bytes=VMEM_LIMIT),
        cost_estimate=estimate(28_000_000_000),
        name="backward",
    )(d_out, g1, g2, *held, *ins, *(kept if threaded else ()))
    return outs[HELD], outs[:HELD], outs[HELD + 1:]


def near_first(part):
    return part in (1, 4, 7)


def place_of(shard, swapped):
    x, near, far = (shard >> 1) & 1, (shard >> 2) & 1, (shard >> 3) & 1
    return (near, 2 * far + x) if swapped else (x, 2 * near + far)


def gradients_kernel(units, parts, gain_ref, arrays, q_ref, p_ref, n_ref, u_ref, d_ref, *scratch):
    a, b, o, packed, got0, got1, got2, got3, isem, ssem, rsem = scratch
    width = p_ref.shape[1]
    share = width // SHARDS
    tokens = a.shape[1] * a.shape[2]
    count = len(parts)
    index = lax.axis_index("dp")
    bits = [lax.rem(index // (1 << k), 2) for k in range(4)]

    def partner(k):
        return {"dp": index + (1 << k) * (1 - 2 * bits[k])}

    barrier = pltpu.get_barrier_semaphore()
    for k in range(4):
        pl.semaphore_signal(barrier, inc=1, device_id=partner(k), device_id_type=MESH)

    def loads(i):
        left, left_at, right, right_at = units[i][:4]
        from_left = arrays[left].at[:, :, pl.ds(left_at * width, width)]
        from_right = arrays[right].at[:, :, pl.ds(right_at * width, width)]
        return (
            pltpu.make_async_copy(from_left, a.at[i % 2], isem.at[0, i % 2]),
            pltpu.make_async_copy(from_right, b.at[i % 2], isem.at[1, i % 2]),
        )

    def rows_of(t):
        return pl.ds(t * share, share + (16 if t == count - 1 else 0))

    def order(t):
        return (0, 2, 3, 1) if near_first(t) else (0, 1, 2, 3)

    def send(t, stage):
        rows = rows_of(t)
        first, second, third = [bits[k] for k in order(t)[1:]]
        if stage == 0:
            src, dst = packed.at[1, :, :, rows], got0.at[:, :, rows]
        elif stage == 1:
            src, dst = packed.at[0, 1 - first, :, rows], got1.at[:, rows]
        elif stage == 2:
            src, dst = packed.at[0, first, pl.ds(2 * (1 - second), 2), rows], got2.at[:, rows]
        else:
            src, dst = packed.at[0, first, 2 * second + 1 - third, rows], got3.at[rows]
        return pltpu.make_async_remote_copy(
            src_ref=src,
            dst_ref=dst,
            send_sem=ssem.at[stage, t],
            recv_sem=rsem.at[stage, t],
            device_id=partner(order(t)[stage]),
            device_id_type=MESH,
        )

    def added(first, second, rows, ref, at):
        total = packed[0, first, second, rows].astype(F32) + ref[at + (rows,)].astype(F32)
        packed[0, first, second, rows] = total.astype(BF)

    def combine(t, stage):
        rows = rows_of(t)
        first, second, third = [bits[k] for k in order(t)[1:]]
        send(t, stage).wait_recv()
        if stage == 0:
            for i in range(2):

                @pl.loop(0, 4)
                def _(j):
                    added(i, j, rows, got0, (i, j))

        elif stage == 1:

            @pl.loop(0, 4)
            def _(j):
                added(first, j, rows, got1, (j,))

        else:
            for i in range(2):
                added(first, 2 * second + i, rows, got2, (i,))
        send(t, stage + 1).start()

    def finish(t):
        rows = rows_of(t)
        first, second, third = [bits[k] for k in order(t)[1:]]
        send(t, 3).wait_recv()
        total = packed[0, first, 2 * second + third, rows].astype(F32) + got3[rows].astype(F32)
        kind, at = parts[t]
        if kind == "down":
            d_ref[at * share:(at + 1) * share] = total
        elif kind == "up":
            u_ref[:, at * width:(at + 1) * width] = total
        elif kind == "qkv":
            q_ref[:, at * width:(at + 1) * width] = total
        else:
            p_ref[...] = total[:share]
            for d in range(SHARDS):

                @pl.when(index == d)
                def _():
                    n_ref[...] = total[share:, d * share:(d + 1) * share]


    def place(d, t):
        first, rest = place_of(d, near_first(t))
        return lax.rem(bits[0] + d % 2, 2), first, rest, slice(t * share, (t + 1) * share)

    def produce(i):
        for copy in loads(i):
            copy.wait()
        if i + 1 < len(units):
            for copy in loads(i + 1):
                copy.start()
        kind, at = units[i][4:]

        @pl.loop(0, width // 256)
        def _(step):
            lanes = pl.ds(pl.multiple_of(step * 256, 256), 256)
            tile = a[i % 2, :, :, lanes].reshape(tokens, 256)
            o[lanes, :] = dot_tn(tile, b[i % 2].reshape(tokens, width)).astype(BF)

        if kind == "down":
            for d in range(4 * at, 4 * at + 4):
                for s in range(4):
                    base = (d % 4 * 4 + s) * share
                    packed[place(d, parts.index(("down", s)))] = o[base:base + share]
        else:
            for d in range(SHARDS):
                packed[place(d, parts.index((kind, at)))] = o[d * share:(d + 1) * share]
        if kind == "proj":
            row = lax.broadcasted_iota(jnp.int32, (16, width), 0)
            both = gain_ref[0] + gain_ref[1]
            upper = jnp.sum(both[0:8], axis=0, keepdims=True)
            lower = jnp.sum(both[8:16], axis=0, keepdims=True)
            gain = jnp.where(row == 0, upper, jnp.where(row == 1, lower, 0.0)).astype(BF)
            for side in range(2):
                for d in range(SHARDS // 2):
                    packed[side, d // 4, d % 4, count * share:count * share + 16] = gain

    for copy in loads(0):
        copy.start()
    pl.semaphore_wait(barrier, 4)
    ready = 0
    for step in range(count + 3 * LAG + 1):
        while ready < min(len(units), 2 * step + 1 if step < 5 else step + 5):
            produce(ready)
            ready += 1
        if step < count:
            send(step, 0).start()
        for stage, t in enumerate((step - 1, step - 1 - LAG, step - 1 - 2 * LAG)):
            if 0 <= t < count:
                combine(t, stage)
        if 0 <= step - 1 - 3 * LAG < count:
            finish(step - 1 - 3 * LAG)
    for t in range(count):
        for stage in range(4):
            send(t, stage).wait_send()


def gradients(act, d_branch, nm, d_up, xn, d_qkv, mix, d_proj_in, gains):
    rows, width = d_branch.shape[1:]
    hidden = act.shape[2]
    share = width // SHARDS
    arrays = (act, d_branch, nm, d_up, xn, d_qkv, mix, d_proj_in)
    n = len(arrays)
    up = [(2, 0, 3, j, "up", j) for j in range(4)]
    down = [(0, j, 1, 0, "down", j) for j in range(4)]
    qkv = [(4, 0, 5, j, "qkv", j) for j in range(3)]
    proj = [(6, 0, 7, 0, "proj", 0)]
    units = [up[0], up[1], down[0], up[2], down[1], up[3], down[2], qkv[0], down[3], qkv[1], qkv[2], proj[0]]
    parts = [u[4:] for u in up + qkv[:1] + down + qkv[1:] + proj]
    total = len(parts) * share + 16

    def kernel(*refs):
        gradients_kernel(units, parts, refs[n], refs[:n], *refs[n + 1:])

    return pl.pallas_call(
        kernel,
        out_shape=[
            jax.ShapeDtypeStruct((share, 3 * width), F32),
            jax.ShapeDtypeStruct((share, width), F32),
            jax.ShapeDtypeStruct((16, share), F32),
            jax.ShapeDtypeStruct((share, hidden), F32),
            jax.ShapeDtypeStruct((hidden // SHARDS, width), F32),
        ],
        in_specs=[ANY] * n + [VM],
        out_specs=[VM] * 5,
        scratch_shapes=[
            pltpu.VMEM((2, 2, rows, width), BF),
            pltpu.VMEM((2, 2, rows, width), BF),
            pltpu.VMEM((width, width), BF),
            pltpu.VMEM((2, 2, 4, total, width), BF),
            pltpu.VMEM((2, 4, total, width), BF),
            pltpu.VMEM((4, total, width), BF),
            pltpu.VMEM((2, total, width), BF),
            pltpu.VMEM((total, width), BF),
            pltpu.SemaphoreType.DMA((2, 2)),
            pltpu.SemaphoreType.DMA((4, len(parts))),
            pltpu.SemaphoreType.DMA((4, len(parts))),
        ],
        compiler_params=pltpu.CompilerParams(vmem_limit_bytes=58 << 20, collective_id=0, has_side_effects=True),
        cost_estimate=estimate(60_000_000_000),
        name="gradients",
    )(*arrays, gains)


def over_tokens(left, right):
    grad = lax.dot_general(left, right, (((0, 1), (0, 1)), ((), ())), preferred_element_type=F32)
    return grad.astype(BF)


def swap(value, bit, count):
    return lax.ppermute(value, "dp", [(i, i ^ bit) for i in range(count)])


def halving_sum(grad, count):
    index = lax.axis_index("dp")
    bit = 1
    while bit < count:
        mine = (index // bit) % 2
        pieces = grad.reshape((grad.shape[0] // 2, 2) + grad.shape[1:])
        sent = lax.dynamic_index_in_dim(pieces, 1 - mine, 1, keepdims=False)
        held = lax.dynamic_index_in_dim(pieces, mine, 1, keepdims=False)
        total = held.astype(F32) + swap(sent, bit, count).astype(F32)
        bit *= 2
        grad = total if bit == count else total.astype(BF)
    return grad[0]


def scattered(grad, count):
    return halving_sum(grad.reshape((count, grad.shape[0] // count) + grad.shape[1:]), count)


def on_device(inputs, video_ids, view_ids, attn_gain, mlp_gain, w_qkv, w_proj, w_up, w_down, out_grad):
    count = lax.axis_size("dp")
    rows, width = inputs.shape
    held = (w_qkv, w_proj, w_up, w_down)
    video, view = video_ids.reshape(1, rows), view_ids.reshape(1, rows)
    gains = (attn_gain, mlp_gain)

    saved = None
    arrived = []
    for block in (0, 1):
        out, held, saved = forward(block, 0, inputs, video, view, *gains, held, saved)
        arrived.append(lax.ppermute(out, "section", [(0, 1)]))
    for block in (0, 1):
        _, held, saved = forward(block, 1, arrived[block], video, view, *gains, held, saved)
    kept = None
    came = []
    for block in (0, 1):
        d_in, held, kept = backward(block, 1, out_grad, *gains, held, saved, kept)
        came.append(lax.ppermute(d_in, "section", [(1, 0)]))
    for block in (0, 1):
        _, held, kept = backward(block, 0, came[block], *gains, held, saved, kept)
    h, xn, qkv, x, mix, lin, aft, nm, act, layer_outputs = saved
    d_branch, d_up, d_proj_in, d_qkv, gain_grads, input_grads = kept

    hidden = w_up.shape[2]
    share = width // count
    if count == SHARDS and hidden == 4 * width:
        g_qkv, g_proj, gain_rows, g_up, g_down = gradients(
            act, d_branch, nm, d_up, xn, d_qkv, mix, d_proj_in, gain_grads
        )
        gain_sums = gain_rows[:2]
    else:
        g_down = scattered(over_tokens(act, d_branch), count)
        g_up = scattered(over_tokens(nm, d_up), count)
        g_proj = over_tokens(mix, d_proj_in).reshape(count, share, width)
        g_qkv = scattered(over_tokens(xn, d_qkv), count)
        gain_sums = gain_grads.reshape(2, 2, 8, width).sum((0, 2)).reshape(2, count, share)
        gain_sums = jnp.pad(gain_sums.transpose(1, 0, 2), ((0, 0), (0, 14), (0, width - share))).astype(BF)
        joined = halving_sum(jnp.concatenate([g_proj, gain_sums], axis=1), count)
        g_proj, gain_sums = joined[:share], joined[share:share + 2, :share]
    return (
        layer_outputs.reshape(1, rows, width),
        input_grads.reshape(1, rows, width),
        gain_sums[0:1],
        gain_sums[1:2],
        g_qkv[None],
        g_proj[None],
        g_up[None],
        g_down[None],
    )


def solution(mesh):
    in_specs = (
        P("dp", None),
        P("dp"),
        P("dp"),
        P("section", None),
        P("section", None),
        P("section", None, None),
        P("section", None, None),
        P("section", None, None),
        P("section", None, None),
        P("dp", None),
    )
    out_specs = (
        P("section", "dp", None),
        P("section", "dp", None),
        P("section", "dp"),
        P("section", "dp"),
        P("section", "dp", None),
        P("section", "dp", None),
        P("section", "dp", None),
        P("section", "dp", None),
    )
    return jax.shard_map(on_device, mesh=mesh, in_specs=in_specs, out_specs=out_specs, check_vma=False)
```

```python
import functools

import jax
import jax.numpy as jnp
from jax import lax
from jax.experimental import pallas as pl
from jax.experimental.pallas import tpu as pltpu
from jax.sharding import PartitionSpec as P

BF = jnp.bfloat16
F32 = jnp.float32
HEAD_DIM = 64
MB_ROWS = 512
EPSILON = 1e-6
NEG_FILL = -1e30
C0 = 0.7978845608028654
C1 = 0.044715
LANES = 128
VMEM_LIMIT = 43 << 20
HELD = 5
SHARDS = 16
LAG = 2
ROW_PART = 256

VM = pl.BlockSpec(memory_space=pltpu.VMEM)
ANY = pl.BlockSpec(memory_space=pl.ANY)
MESH = pl.DeviceIdType.MESH


def dot_nn(a, b):
    return jnp.dot(a, b, preferred_element_type=F32)


def dot_nt(a, b):
    return lax.dot_general(a, b, (((1,), (1,)), ((), ())), preferred_element_type=F32)


def dot_tn(a, b):
    return lax.dot_general(a, b, (((0,), (0,)), ((), ())), preferred_element_type=F32)


def normalized(x):
    center = x - jnp.mean(x, axis=-1, keepdims=True)
    inv = lax.rsqrt(jnp.mean(center * center, axis=-1, keepdims=True) + EPSILON)
    return center * inv, inv


def norm_back(d_hat, hat, inv):
    first = jnp.mean(d_hat, axis=-1, keepdims=True)
    second = jnp.mean(d_hat * hat, axis=-1, keepdims=True)
    return inv * (d_hat - first - hat * second)


def folded_rows(x):
    rows, width = x.shape
    return jnp.sum(x.reshape(rows // 8, 8, width), axis=0)


def row_parts(rows):
    return [slice(i * ROW_PART, (i + 1) * ROW_PART) for i in range(rows // ROW_PART)]


def gelu_and_slope(u):
    a = C0 * u
    b = a * (C1 * (u * u))
    gate = 0.5 + 0.5 * jnp.tanh(a + b)
    return u * gate, gate + (gate - gate * gate) * (2.0 * a + 6.0 * b)


def in_half(lane, half, inside, outside):
    return jnp.where((lane < 64) if half == 0 else (lane >= 64), inside, outside)


def kept_shapes(rows, width, hidden):
    heads = width // HEAD_DIM
    shapes = [
        ((rows, width), BF),
        ((rows, width), BF),
        ((rows, 3 * width), BF),
        ((heads, rows, rows), BF),
        ((rows, width), BF),
        ((rows, width), F32),
        ((rows, width), F32),
        ((rows, width), BF),
        ((rows, hidden), BF),
        ((rows, width), BF),
    ]
    return shapes


def forward_kernel(UNROLL, FT, block, stage, h_h, vid_ref, view_ref, g1_ref, g2_ref, *rest):
    count = len(kept_shapes(1, HEAD_DIM, 1))
    loading = (block, stage) == (0, 0)
    sources = rest[:4]
    rest = rest[4 if loading else HELD + count:]
    wq, wp, wu, wd, gp = rest[:HELD]
    o_h = rest[HELD]
    rest = rest[1 + HELD:]
    h_k, xn_h, qkv_h, x_h, mix_h, lin_h, aft_h, nm_h, act_h, out_h = rest[:count]
    h, xn, qkv, pb, mix, lin, aft, nm, act, low = rest[count:2 * count]
    isem, wsem, osem = rest[2 * count:]
    rows, width = h.shape
    hidden = wu.shape[1]
    pairs = width // LANES
    section = lax.axis_index("section")
    loads = []
    if loading:
        loads = [pltpu.make_async_copy(a.at[0], b, wsem.at[i]) for i, (a, b) in enumerate(zip(sources, (wq, wp, wu, wd)))]
        loads[0].start()

    @pl.when(section == stage)
    def _():
        fetch = pltpu.make_async_copy(h_h if stage else h_h.at[pl.ds(block * rows, rows)], h, isem)
        fetch.start()

        def out(i, src, dst):
            copy = pltpu.make_async_copy(src, dst, osem.at[i])
            copy.start()
            return copy

        here = pl.ds(block * rows, rows)
        video = vid_ref[:, here]
        view = view_ref[:, here]
        code = (video - video[:, :1]) * 4 + view
        place = lax.broadcasted_iota(jnp.int32, (LANES, rows), 0) % 64
        query_code = jnp.where(place == code - section, 1.0, 0.0).astype(BF).T
        key_code = jnp.where((place == code) | (place >= 8), 0.0, NEG_FILL).astype(BF).T
        live = jnp.broadcast_to(jnp.where(view >= section, 1.0, 0.0), (LANES, rows)).T
        fetch.wait()
        if loading:
            loads[0].wait()
            for copy in loads[1:]:
                copy.start()
        for r in row_parts(rows):
            xn[r] = (normalized(h[r].astype(F32))[0] * g1_ref[...]).astype(BF)
            for t in range(3):
                cols = slice(t * width, (t + 1) * width)
                qkv[r, cols] = dot_nn(xn[r], wq[:, cols]).astype(BF)
        copies = [out(1, xn, xn_h.at[block])]
        copies.append(out(2, qkv, qkv_h.at[block]))
        tiles = hidden // FT
        copies.append(out(0, h, h_k.at[block]))
        lane = lax.broadcasted_iota(jnp.int32, (1, LANES), 1)

        @pl.loop(0, pairs // UNROLL)
        def _(step):
            pair = [step * UNROLL + u for u in range(UNROLL)]
            col = [pl.multiple_of(p * LANES, LANES) for p in pair]

            def scores(u, e):
                q = qkv[:, pl.ds(col[u], LANES)] * jnp.asarray(0.125, BF)
                k = qkv[:, pl.ds(width + col[u], LANES)]
                return dot_nt(in_half(lane, e, q, query_code), in_half(lane, e, k, key_code))

            def mixed(u, e, s):
                top = jnp.max(s, axis=-1, keepdims=True)
                x = jnp.exp(s - top).astype(BF)
                pb[2 * pair[u] + e] = x
                v = qkv[:, pl.ds(2 * width + col[u], LANES)]
                return dot_nn(x, in_half(lane, e, v, jnp.ones_like(v)))

            items = [(u, e) for u in range(UNROLL) for e in (0, 1)]
            s = scores(*items[0])
            parts = []
            for i, (u, e) in enumerate(items):
                following = scores(*items[i + 1]) if i + 1 < len(items) else None
                parts.append(mixed(u, e, s))
                s = following
            for u in range(UNROLL):
                a, b = parts[2 * u:2 * u + 2]
                scale = live / pltpu.roll(jnp.where(lane < 64, b, a), 64, 1)
                lin[:, pl.ds(col[u], LANES)] = scale
                mix[:, pl.ds(col[u], LANES)] = (jnp.where(lane < 64, a, b) * scale).astype(BF)
            heads = pl.ds(2 * UNROLL * step, 2 * UNROLL)
            pltpu.make_async_copy(pb.at[heads], x_h.at[block, heads], osem.at[3]).start()

        copies.append(out(4, mix, mix_h.at[block]))
        copies.append(out(5, lin, lin_h.at[block]))
        if loading:
            loads[1].wait()
        for r in row_parts(rows):
            after = h[r].astype(F32) + dot_nn(mix[r], wp[...])
            aft[r] = after
            nm[r] = (normalized(after)[0] * g2_ref[...]).astype(BF)
        copies.append(out(6, aft, aft_h.at[block]))
        copies.append(out(7, nm, nm_h.at[block]))

        def up(t):
            return dot_nn(nm[...], wu[:, t * FT:(t + 1) * FT])

        if loading:
            loads[2].wait()
            loads[3].wait()
        u = up(0)
        total = None
        for t in range(tiles):
            following = up(t + 1) if t + 1 < tiles else None
            value, slope = gelu_and_slope(u)
            cols = slice(t * FT, (t + 1) * FT)
            value = value.astype(BF)
            act[:, cols] = value
            gp[block, :, cols] = slope.astype(BF)
            if t == tiles // 2:
                part = slice(0, t * FT)
                pltpu.make_async_copy(act.at[:, part], act_h.at[block, :, part], osem.at[8]).start()
            term = dot_nn(value, wd[cols, :])
            total = term if total is None else total + term
            u = following
        part = slice(tiles // 2 * FT, hidden)
        pltpu.make_async_copy(act.at[:, part], act_h.at[block, :, part], osem.at[8]).start()
        result = (aft[...] + total).astype(BF)
        low[...] = result
        copies.append(out(9, low, out_h.at[block]))
        copies.append(out(10, low, o_h))
        pltpu.make_async_copy(act, act_h.at[block], osem.at[8]).wait()
        pltpu.make_async_copy(pb, x_h.at[block], osem.at[3]).wait()
        for copy in copies:
            copy.wait()

    if loading:

        @pl.when(section != stage)
        def _():
            loads[0].wait()
            for copy in loads[1:]:
                copy.start()
            for copy in loads[1:]:
                copy.wait()


def estimate(flops):
    return pl.CostEstimate(flops=flops, bytes_accessed=30 << 20, transcendentals=0)


def held_shapes(weights):
    rows, hidden = MB_ROWS, weights[2].shape[-1]
    return [pltpu.VMEM(w.shape[-2:], BF) for w in weights[:4]] + [pltpu.VMEM((2, rows, hidden), BF)]


def forward(block, stage, h, video, view, g1, g2, held, kept):
    rows, width, hidden = MB_ROWS, h.shape[1], held[2].shape[-1]
    shapes = kept_shapes(rows, width, hidden)
    n = len(shapes)
    threaded = kept is not None
    outs = pl.pallas_call(
        functools.partial(forward_kernel, 2, 512, block, stage),
        out_shape=held_shapes(held)
        + [jax.ShapeDtypeStruct((rows, width), BF)]
        + [jax.ShapeDtypeStruct((2,) + s, d) for s, d in shapes],
        in_specs=[ANY] + [VM] * 4 + ([VM] * HELD + [ANY] * n if threaded else [ANY] * 4),
        out_specs=[VM] * HELD + [ANY] * (n + 1),
        scratch_shapes=[pltpu.VMEM(s, d) for s, d in shapes]
        + [pltpu.SemaphoreType.DMA, pltpu.SemaphoreType.DMA((4,)), pltpu.SemaphoreType.DMA((n + 1,))],
        input_output_aliases={5 + i: i + (i >= HELD) for i in range(HELD + n)} if threaded else {},
        compiler_params=pltpu.CompilerParams(vmem_limit_bytes=VMEM_LIMIT),
        cost_estimate=estimate(25_000_000_000),
        name="forward",
    )(h, video, view, g1, g2, *held, *(kept if threaded else ()))
    return outs[HELD], outs[:HELD], outs[HELD + 1:]


def backward_shapes(rows, width, hidden):
    return [
        ((rows, width), BF),
        ((rows, hidden), BF),
        ((rows, width), BF),
        ((rows, 3 * width), BF),
        ((16, width), F32),
        ((rows, width), BF),
    ]


def backward_kernel(UNROLL, FT, block, stage, do_h, g1_ref, g2_ref, *rest):
    n = len(backward_shapes(1, 1, 1))
    h_k, qkv_h, x_h, mix_h, lin_h, aft_h = rest[HELD:HELD + 6]
    rest = rest[HELD + 6 + (0 if (block, stage) == (0, 1) else n):]
    wq, wp, wu, wd, gp = rest[:HELD]
    sent_h = rest[HELD]
    rest = rest[HELD + 1:]
    do_k, dup_h, dpi_h, dqkv_h, gain_h, dh_h = rest[:n]
    do, dup, dpi, dqkv, gain, low = rest[n:2 * n]
    h, qkv, x, mix, lin, aft, dos, qt, ot, da, isem, osem = rest[2 * n:]
    rows, width = h.shape
    hidden = wu.shape[1]
    pairs = width // LANES
    tiles = hidden // FT

    @pl.when(lax.axis_index("section") == stage)
    def _():
        sources = (
            (do_h.at[pl.ds(block * rows, rows)] if stage else do_h, do),
            (aft_h.at[block], aft),
            (lin_h.at[block], lin),
            (mix_h.at[block], mix),
            (qkv_h.at[block], qkv),
            (x_h.at[block], x),
            (h_k.at[block], h),
        )
        loads = [pltpu.make_async_copy(a, b, isem.at[i]) for i, (a, b) in enumerate(sources)]
        for copy in loads:
            copy.start()

        def out(i, src, dst):
            copy = pltpu.make_async_copy(src, dst, osem.at[i])
            copy.start()
            return copy

        loads[0].wait()
        d_out = do[...]

        def down(t):
            return dot_nt(d_out, wd[t * FT:(t + 1) * FT, :])

        u = down(0)
        total = None
        for t in range(tiles):
            following = down(t + 1) if t + 1 < tiles else None
            cols = slice(t * FT, (t + 1) * FT)
            value = (u * gp[block, :, cols].astype(F32)).astype(BF)
            dup[:, cols] = value
            term = dot_nt(value, wu[:, cols])
            total = term if total is None else total + term
            u = following
        copies = [out(0, do, do_k.at[block]), out(1, dup, dup_h.at[block])]
        loads[1].wait()
        hat, inv = normalized(aft[...])
        gain[8:16] = folded_rows(total * hat)
        d_after = d_out.astype(F32) + norm_back(total * g2_ref[...], hat, inv)
        da[...] = d_after
        dpi[...] = d_after.astype(BF)
        copies.append(out(2, dpi, dpi_h.at[block]))
        lane = lax.broadcasted_iota(jnp.int32, (1, LANES), 1)
        row = lax.broadcasted_iota(jnp.int32, (LANES, LANES), 0)
        column = lax.broadcasted_iota(jnp.int32, (LANES, LANES), 1)
        across = jnp.where((row < 64) != (column < 64), -1.0, 0.0).astype(BF)
        for copy in loads[2:]:
            copy.wait()
        dos[...] = (dot_nt(dpi[...], wp[...]) * lin[...]).astype(BF)
        for p in range(pairs):
            cols = slice(p * LANES, (p + 1) * LANES)
            qt[cols] = qkv[:, cols].T
            ot[cols] = dos[:, cols].T

        @pl.loop(0, pairs // UNROLL)
        def _(step):
            pair = [step * UNROLL + u for u in range(UNROLL)]
            col = [pl.multiple_of(p * LANES, LANES) for p in pair]

            def row_sums(u):
                here = pl.ds(col[u], LANES)
                product = dos[:, here].astype(F32) * mix[:, here].astype(F32)
                high = product.astype(BF)
                lower = (product - high.astype(F32)).astype(BF)
                negated = dot_nn(high, across) + dot_nn(lower, across)
                high = negated.astype(BF)
                lower = (negated - high.astype(F32)).astype(BF)
                place = lane % 64
                return jnp.where(place == 0, high, jnp.where(place == 1, lower, jnp.zeros_like(high)))

            sums = [row_sums(u) for u in range(UNROLL)]

            def d_scaled(u, e):
                d_mix = dos[:, pl.ds(col[u], LANES)]
                v = qkv[:, pl.ds(2 * width + col[u], LANES)]
                return dot_nt(in_half(lane, e, d_mix, sums[u]), in_half(lane, e, v, jnp.ones_like(v)))

            items = [(u, e) for u in range(UNROLL) for e in (0, 1)]
            s = d_scaled(*items[0])
            results = []
            for i, (u, e) in enumerate(items):
                following = d_scaled(*items[i + 1]) if i + 1 < len(items) else None
                weights = x[2 * pair[u] + e]
                d_scores = (weights.astype(F32) * s).astype(BF)
                k = qkv[:, pl.ds(width + col[u], LANES)]
                d_query = dot_nn(d_scores, in_half(lane, e, k, jnp.zeros_like(k)))
                head = pl.ds(pl.multiple_of(col[u] + 64 * e, 64), 64)
                results.append((d_query, dot_nn(qt[head], d_scores), dot_nn(ot[head], weights)))
                s = following
            for u in range(UNROLL):
                a, b = results[2 * u:2 * u + 2]
                dqkv[:, pl.ds(col[u], LANES)] = ((a[0] + b[0]) * 0.125).astype(BF)
                d_key = jnp.concatenate([a[1], b[1]], axis=0) * 0.125
                dqkv[:, pl.ds(width + col[u], LANES)] = d_key.astype(BF).T
                d_value = jnp.concatenate([a[2], b[2]], axis=0)
                dqkv[:, pl.ds(2 * width + col[u], LANES)] = d_value.astype(BF).T

        copies.append(out(3, dqkv, dqkv_h.at[block]))
        total = None
        for t in range(3):
            cols = slice(t * width, (t + 1) * width)
            term = dot_nt(dqkv[:, cols], wq[:, cols])
            total = term if total is None else total + term
        hat, inv = normalized(h[...].astype(F32))
        gain[0:8] = folded_rows(total * hat)
        copies.append(out(4, gain, gain_h.at[block]))
        result = (da[...] + norm_back(total * g1_ref[...], hat, inv)).astype(BF)
        low[...] = result
        copies.append(out(5, low, dh_h.at[block]))
        copies.append(out(6, low, sent_h))
        for copy in copies:
            copy.wait()


def backward(block, stage, d_out, g1, g2, held, saved, kept):
    rows, width, hidden = MB_ROWS, d_out.shape[1], held[2].shape[-1]
    shapes = backward_shapes(rows, width, hidden)
    n = len(shapes)
    threaded = kept is not None
    h, xn, qkv, x, mix, lin, aft, nm, act, produced = saved
    ins = (h, qkv, x, mix, lin, aft)
    aliases = {3 + i: i for i in range(HELD)}
    if threaded:
        aliases.update({3 + HELD + len(ins) + i: HELD + 1 + i for i in range(n)})
    outs = pl.pallas_call(
        functools.partial(backward_kernel, 2, 512, block, stage),
        out_shape=held_shapes(held)
        + [jax.ShapeDtypeStruct((rows, width), BF)]
        + [jax.ShapeDtypeStruct((2,) + s, d) for s, d in shapes],
        in_specs=[ANY] + [VM] * (2 + HELD) + [ANY] * (len(ins) + (n if threaded else 0)),
        out_specs=[VM] * HELD + [ANY] * (n + 1),
        scratch_shapes=[pltpu.VMEM(s, d) for s, d in shapes]
        + [pltpu.VMEM(a.shape[1:], a.dtype) for a in ins]
        + [pltpu.VMEM((rows, width), BF), pltpu.VMEM((width, rows), BF), pltpu.VMEM((width, rows), BF)]
        + [pltpu.VMEM((rows, width), F32)]
        + [pltpu.SemaphoreType.DMA((len(ins) + 1,)), pltpu.SemaphoreType.DMA((n + 1,))],
        input_output_aliases=aliases,
        compiler_params=pltpu.CompilerParams(vmem_limit_bytes=VMEM_LIMIT),
        cost_estimate=estimate(28_000_000_000),
        name="backward",
    )(d_out, g1, g2, *held, *ins, *(kept if threaded else ()))
    return outs[HELD], outs[:HELD], outs[HELD + 1:]


def near_first(part):
    return part in (3, 7)


def place_of(shard, swapped):
    x, near, far = (shard >> 1) & 1, (shard >> 2) & 1, (shard >> 3) & 1
    return (near, 2 * far + x) if swapped else (x, 2 * near + far)


def gradients_kernel(units, parts, gain_ref, arrays, q_ref, p_ref, n_ref, u_ref, d_ref, *scratch):
    a, b, o, packed, got0, got1, got2, got3, isem, ssem, rsem = scratch
    width = p_ref.shape[1]
    share = width // SHARDS
    tokens = a.shape[1] * a.shape[2]
    count = len(parts)
    index = lax.axis_index("dp")
    bits = [lax.rem(index // (1 << k), 2) for k in range(4)]

    def partner(k):
        return {"dp": index + (1 << k) * (1 - 2 * bits[k])}

    barrier = pltpu.get_barrier_semaphore()
    for k in range(4):
        pl.semaphore_signal(barrier, inc=1, device_id=partner(k), device_id_type=MESH)

    def loads(i):
        left, left_at, right, right_at = units[i][:4]
        from_left = arrays[left].at[:, :, pl.ds(left_at * width, width)]
        from_right = arrays[right].at[:, :, pl.ds(right_at * width, width)]
        return (
            pltpu.make_async_copy(from_left, a.at[i % 2], isem.at[0, i % 2]),
            pltpu.make_async_copy(from_right, b.at[i % 2], isem.at[1, i % 2]),
        )

    def rows_of(t):
        return pl.ds(t * share, share + (16 if t == count - 1 else 0))

    def order(t):
        return (0, 2, 3, 1) if near_first(t) else (0, 1, 2, 3)

    def send(t, stage):
        rows = rows_of(t)
        first, second, third = [bits[k] for k in order(t)[1:]]
        if stage == 0:
            src, dst = packed.at[1, :, :, rows], got0.at[:, :, rows]
        elif stage == 1:
            src, dst = packed.at[0, 1 - first, :, rows], got1.at[:, rows]
        elif stage == 2:
            src, dst = packed.at[0, first, pl.ds(2 * (1 - second), 2), rows], got2.at[:, rows]
        else:
            src, dst = packed.at[0, first, 2 * second + 1 - third, rows], got3.at[rows]
        return pltpu.make_async_remote_copy(
            src_ref=src,
            dst_ref=dst,
            send_sem=ssem.at[stage, t],
            recv_sem=rsem.at[stage, t],
            device_id=partner(order(t)[stage]),
            device_id_type=MESH,
        )

    def added(first, second, rows, ref, at):
        total = packed[0, first, second, rows].astype(F32) + ref[at + (rows,)].astype(F32)
        packed[0, first, second, rows] = total.astype(BF)

    def combine(t, stage):
        rows = rows_of(t)
        first, second, third = [bits[k] for k in order(t)[1:]]
        send(t, stage).wait_recv()
        if stage == 0:
            for i in range(2):

                @pl.loop(0, 4)
                def _(j):
                    added(i, j, rows, got0, (i, j))

        elif stage == 1:

            @pl.loop(0, 4)
            def _(j):
                added(first, j, rows, got1, (j,))

        else:
            for i in range(2):
                added(first, 2 * second + i, rows, got2, (i,))
        send(t, stage + 1).start()

    def finish(t):
        rows = rows_of(t)
        first, second, third = [bits[k] for k in order(t)[1:]]
        send(t, 3).wait_recv()
        total = packed[0, first, 2 * second + third, rows].astype(F32) + got3[rows].astype(F32)
        kind, at = parts[t]
        if kind == "down":
            d_ref[at * share:(at + 1) * share] = total
        elif kind == "up":
            u_ref[:, at * width:(at + 1) * width] = total
        elif kind == "qkv":
            q_ref[:, at * width:(at + 1) * width] = total
        else:
            p_ref[...] = total[:share]
            for d in range(SHARDS):

                @pl.when(index == d)
                def _():
                    n_ref[...] = total[share:, d * share:(d + 1) * share]


    def place(d, t):
        first, rest = place_of(d, near_first(t))
        return lax.rem(bits[0] + d % 2, 2), first, rest, slice(t * share, (t + 1) * share)

    def produce(i):
        for copy in loads(i):
            copy.wait()
        if i + 1 < len(units):
            for copy in loads(i + 1):
                copy.start()
        kind, at = units[i][4:]

        @pl.loop(0, width // 256)
        def _(step):
            lanes = pl.ds(pl.multiple_of(step * 256, 256), 256)
            tile = a[i % 2, :, :, lanes].reshape(tokens, 256)
            o[lanes, :] = dot_tn(tile, b[i % 2].reshape(tokens, width)).astype(BF)

        if kind == "down":
            for d in range(4 * at, 4 * at + 4):
                for s in range(4):
                    base = (d % 4 * 4 + s) * share
                    packed[place(d, parts.index(("down", s)))] = o[base:base + share]
        else:
            for d in range(SHARDS):
                packed[place(d, parts.index((kind, at)))] = o[d * share:(d + 1) * share]
        if kind == "proj":
            row = lax.broadcasted_iota(jnp.int32, (16, width), 0)
            both = gain_ref[0] + gain_ref[1]
            upper = jnp.sum(both[0:8], axis=0, keepdims=True)
            lower = jnp.sum(both[8:16], axis=0, keepdims=True)
            gain = jnp.where(row == 0, upper, jnp.where(row == 1, lower, 0.0)).astype(BF)
            for side in range(2):
                for d in range(SHARDS // 2):
                    packed[side, d // 4, d % 4, count * share:count * share + 16] = gain

    for copy in loads(0):
        copy.start()
    pl.semaphore_wait(barrier, 4)
    ready = 0
    for step in range(count + 3 * LAG + 1):
        while ready < ([1, 2, 4, 6, 8, 9, 10, 11, 12] + [len(units)] * 40)[step]:
            produce(ready)
            ready += 1
        if step < count:
            send(step, 0).start()
        for stage, t in enumerate((step - 1, step - 1 - LAG, step - 1 - 2 * LAG)):
            if 0 <= t < count:
                combine(t, stage)
        if 0 <= step - 1 - 3 * LAG < count:
            finish(step - 1 - 3 * LAG)
    for t in range(count):
        for stage in range(4):
            send(t, stage).wait_send()


def gradients(act, d_branch, nm, d_up, xn, d_qkv, mix, d_proj_in, gains):
    rows, width = d_branch.shape[1:]
    hidden = act.shape[2]
    share = width // SHARDS
    arrays = (act, d_branch, nm, d_up, xn, d_qkv, mix, d_proj_in)
    n = len(arrays)
    up = [(2, 0, 3, j, "up", j) for j in range(4)]
    down = [(0, j, 1, 0, "down", j) for j in range(4)]
    qkv = [(4, 0, 5, j, "qkv", j) for j in range(3)]
    proj = [(6, 0, 7, 0, "proj", 0)]
    units = [up[0], up[1], down[0], up[2], down[1], up[3], down[2], qkv[0], down[3], qkv[1], qkv[2], proj[0]]
    parts = [u[4:] for u in up + qkv[:1] + down + qkv[1:] + proj]
    total = len(parts) * share + 16

    def kernel(*refs):
        gradients_kernel(units, parts, refs[n], refs[:n], *refs[n + 1:])

    return pl.pallas_call(
        kernel,
        out_shape=[
            jax.ShapeDtypeStruct((share, 3 * width), F32),
            jax.ShapeDtypeStruct((share, width), F32),
            jax.ShapeDtypeStruct((16, share), F32),
            jax.ShapeDtypeStruct((share, hidden), F32),
            jax.ShapeDtypeStruct((hidden // SHARDS, width), F32),
        ],
        in_specs=[ANY] * n + [VM],
        out_specs=[VM] * 5,
        scratch_shapes=[
            pltpu.VMEM((2, 2, rows, width), BF),
            pltpu.VMEM((2, 2, rows, width), BF),
            pltpu.VMEM((width, width), BF),
            pltpu.VMEM((2, 2, 4, total, width), BF),
            pltpu.VMEM((2, 4, total, width), BF),
            pltpu.VMEM((4, total, width), BF),
            pltpu.VMEM((2, total, width), BF),
            pltpu.VMEM((total, width), BF),
            pltpu.SemaphoreType.DMA((2, 2)),
            pltpu.SemaphoreType.DMA((4, len(parts))),
            pltpu.SemaphoreType.DMA((4, len(parts))),
        ],
        compiler_params=pltpu.CompilerParams(vmem_limit_bytes=50 << 20, collective_id=0, has_side_effects=True),
        cost_estimate=estimate(60_000_000_000),
        name="gradients",
    )(*arrays, gains)


def over_tokens(left, right):
    grad = lax.dot_general(left, right, (((0, 1), (0, 1)), ((), ())), preferred_element_type=F32)
    return grad.astype(BF)


def swap(value, bit, count):
    return lax.ppermute(value, "dp", [(i, i ^ bit) for i in range(count)])


def halving_sum(grad, count):
    index = lax.axis_index("dp")
    bit = 1
    while bit < count:
        mine = (index // bit) % 2
        pieces = grad.reshape((grad.shape[0] // 2, 2) + grad.shape[1:])
        sent = lax.dynamic_index_in_dim(pieces, 1 - mine, 1, keepdims=False)
        held = lax.dynamic_index_in_dim(pieces, mine, 1, keepdims=False)
        total = held.astype(F32) + swap(sent, bit, count).astype(F32)
        bit *= 2
        grad = total if bit == count else total.astype(BF)
    return grad[0]


def scattered(grad, count):
    return halving_sum(grad.reshape((count, grad.shape[0] // count) + grad.shape[1:]), count)


def on_device(inputs, video_ids, view_ids, attn_gain, mlp_gain, w_qkv, w_proj, w_up, w_down, out_grad):
    count = lax.axis_size("dp")
    rows, width = inputs.shape
    held = (w_qkv, w_proj, w_up, w_down)
    video, view = video_ids.reshape(1, rows), view_ids.reshape(1, rows)
    gains = (attn_gain, mlp_gain)

    saved = None
    arrived = []
    for block in (0, 1):
        out, held, saved = forward(block, 0, inputs, video, view, *gains, held, saved)
        arrived.append(lax.ppermute(out, "section", [(0, 1)]))
    for block in (0, 1):
        _, held, saved = forward(block, 1, arrived[block], video, view, *gains, held, saved)
    kept = None
    came = []
    for block in (0, 1):
        d_in, held, kept = backward(block, 1, out_grad, *gains, held, saved, kept)
        came.append(lax.ppermute(d_in, "section", [(1, 0)]))
    for block in (0, 1):
        _, held, kept = backward(block, 0, came[block], *gains, held, saved, kept)
    h, xn, qkv, x, mix, lin, aft, nm, act, layer_outputs = saved
    d_branch, d_up, d_proj_in, d_qkv, gain_grads, input_grads = kept

    hidden = w_up.shape[2]
    share = width // count
    if count == SHARDS and hidden == 4 * width:
        g_qkv, g_proj, gain_rows, g_up, g_down = gradients(
            act, d_branch, nm, d_up, xn, d_qkv, mix, d_proj_in, gain_grads
        )
        gain_sums = gain_rows[:2]
    else:
        g_down = scattered(over_tokens(act, d_branch), count)
        g_up = scattered(over_tokens(nm, d_up), count)
        g_proj = over_tokens(mix, d_proj_in).reshape(count, share, width)
        g_qkv = scattered(over_tokens(xn, d_qkv), count)
        gain_sums = gain_grads.reshape(2, 2, 8, width).sum((0, 2)).reshape(2, count, share)
        gain_sums = jnp.pad(gain_sums.transpose(1, 0, 2), ((0, 0), (0, 14), (0, width - share))).astype(BF)
        joined = halving_sum(jnp.concatenate([g_proj, gain_sums], axis=1), count)
        g_proj, gain_sums = joined[:share], joined[share:share + 2, :share]
    return (
        layer_outputs.reshape(1, rows, width),
        input_grads.reshape(1, rows, width),
        gain_sums[0:1],
        gain_sums[1:2],
        g_qkv[None],
        g_proj[None],
        g_up[None],
        g_down[None],
    )


def solution(mesh):
    in_specs = (
        P("dp", None),
        P("dp"),
        P("dp"),
        P("section", None),
        P("section", None),
        P("section", None, None),
        P("section", None, None),
        P("section", None, None),
        P("section", None, None),
        P("dp", None),
    )
    out_specs = (
        P("section", "dp", None),
        P("section", "dp", None),
        P("section", "dp"),
        P("section", "dp"),
        P("section", "dp", None),
        P("section", "dp", None),
        P("section", "dp", None),
        P("section", "dp", None),
    )
    return jax.shard_map(on_device, mesh=mesh, in_specs=in_specs, out_specs=out_specs, check_vma=False)
```

```python
import functools

import jax
import jax.numpy as jnp
from jax import lax
from jax.experimental import pallas as pl
from jax.experimental.pallas import tpu as pltpu
from jax.sharding import PartitionSpec as P

BF = jnp.bfloat16
F32 = jnp.float32
HEAD_DIM = 64
MB_ROWS = 512
EPSILON = 1e-6
NEG_FILL = -1e30
C0 = 0.7978845608028654
C1 = 0.044715
LANES = 128
VMEM_LIMIT = 43 << 20
HELD = 5
SHARDS = 16
LAG = 2
ROW_PART = 256

VM = pl.BlockSpec(memory_space=pltpu.VMEM)
ANY = pl.BlockSpec(memory_space=pl.ANY)
MESH = pl.DeviceIdType.MESH


def dot_nn(a, b):
    return jnp.dot(a, b, preferred_element_type=F32)


def dot_nt(a, b):
    return lax.dot_general(a, b, (((1,), (1,)), ((), ())), preferred_element_type=F32)


def dot_tn(a, b):
    return lax.dot_general(a, b, (((0,), (0,)), ((), ())), preferred_element_type=F32)


def normalized(x):
    center = x - jnp.mean(x, axis=-1, keepdims=True)
    inv = lax.rsqrt(jnp.mean(center * center, axis=-1, keepdims=True) + EPSILON)
    return center * inv, inv


def norm_back(d_hat, hat, inv):
    first = jnp.mean(d_hat, axis=-1, keepdims=True)
    second = jnp.mean(d_hat * hat, axis=-1, keepdims=True)
    return inv * (d_hat - first - hat * second)


def folded_rows(x):
    rows, width = x.shape
    return jnp.sum(x.reshape(rows // 8, 8, width), axis=0)


def row_parts(rows):
    return [slice(i * ROW_PART, (i + 1) * ROW_PART) for i in range(rows // ROW_PART)]


def gelu_and_slope(u):
    a = C0 * u
    b = a * (C1 * (u * u))
    gate = 0.5 + 0.5 * jnp.tanh(a + b)
    return u * gate, gate + (gate - gate * gate) * (2.0 * a + 6.0 * b)


def in_half(lane, half, inside, outside):
    return jnp.where((lane < 64) if half == 0 else (lane >= 64), inside, outside)


def kept_shapes(rows, width, hidden):
    heads = width // HEAD_DIM
    shapes = [
        ((rows, width), BF),
        ((rows, width), BF),
        ((rows, 3 * width), BF),
        ((heads, rows, rows), BF),
        ((rows, width), BF),
        ((rows, width), BF),
        ((rows, width), BF),
        ((rows, width), BF),
        ((rows, hidden), BF),
        ((rows, width), BF),
    ]
    return shapes


def forward_kernel(UNROLL, FT, block, stage, h_h, vid_ref, view_ref, g1_ref, g2_ref, *rest):
    count = len(kept_shapes(1, HEAD_DIM, 1))
    loading = (block, stage) == (0, 0)
    sources = rest[:4]
    rest = rest[4 if loading else HELD + count:]
    wq, wp, wu, wd, gp = rest[:HELD]
    o_h = rest[HELD]
    rest = rest[1 + HELD:]
    h_k, xn_h, qkv_h, x_h, mix_h, lin_h, aft_h, nm_h, act_h, out_h = rest[:count]
    h, xn, qkv, pb, mix, lin, aft, nm, act, low = rest[count:2 * count]
    acc, isem, wsem, osem = rest[2 * count:]
    rows, width = h.shape
    hidden = wu.shape[1]
    pairs = width // LANES
    section = lax.axis_index("section")
    if stage == 1:
        h = h_h
    loads = []
    if loading:
        loads = [pltpu.make_async_copy(a.at[0], b, wsem.at[i]) for i, (a, b) in enumerate(zip(sources, (wq, wp, wu, wd)))]
        loads[0].start()

    @pl.when(section == stage)
    def _():
        fetch = None
        if stage == 0:
            fetch = pltpu.make_async_copy(h_h.at[pl.ds(block * rows, rows)], h, isem)
            fetch.start()

        def out(i, src, dst):
            copy = pltpu.make_async_copy(src, dst, osem.at[i])
            copy.start()
            return copy

        here = pl.ds(block * rows, rows)
        video = vid_ref[:, here]
        view = view_ref[:, here]
        code = (video - video[:, :1]) * 4 + view
        place = lax.broadcasted_iota(jnp.int32, (LANES, rows), 0) % 64
        query_code = jnp.where(place == code - section, 1.0, 0.0).astype(BF).T
        key_code = jnp.where((place == code) | (place >= 8), 0.0, NEG_FILL).astype(BF).T
        live = jnp.broadcast_to(jnp.where(view >= section, 1.0, 0.0), (LANES, rows)).T
        if stage == 0:
            fetch.wait()
        if loading:
            loads[0].wait()
            for copy in loads[1:]:
                copy.start()
        for r in row_parts(rows):
            xn[r] = (normalized(h[r].astype(F32))[0] * g1_ref[...]).astype(BF)
            for t in range(3):
                cols = slice(t * width, (t + 1) * width)
                qkv[r, cols] = dot_nn(xn[r], wq[:, cols]).astype(BF)
        copies = [out(1, xn, xn_h.at[block])]
        copies.append(out(2, qkv, qkv_h.at[block]))
        tiles = hidden // FT
        copies.append(out(0, h, h_k.at[block]))
        lane = lax.broadcasted_iota(jnp.int32, (1, LANES), 1)

        @pl.loop(0, pairs // UNROLL)
        def _(step):
            pair = [step * UNROLL + u for u in range(UNROLL)]
            col = [pl.multiple_of(p * LANES, LANES) for p in pair]

            def scores(u, e):
                q = qkv[:, pl.ds(col[u], LANES)] * jnp.asarray(0.125, BF)
                k = qkv[:, pl.ds(width + col[u], LANES)]
                return dot_nt(in_half(lane, e, q, query_code), in_half(lane, e, k, key_code))

            def mixed(u, e, s):
                top = jnp.max(s, axis=-1, keepdims=True)
                x = jnp.exp(s - top).astype(BF)
                pb[2 * pair[u] + e] = x
                v = qkv[:, pl.ds(2 * width + col[u], LANES)]
                return dot_nn(x, in_half(lane, e, v, jnp.ones_like(v)))

            items = [(u, e) for u in range(UNROLL) for e in (0, 1)]
            s = scores(*items[0])
            parts = []
            for i, (u, e) in enumerate(items):
                following = scores(*items[i + 1]) if i + 1 < len(items) else None
                parts.append(mixed(u, e, s))
                s = following
            for u in range(UNROLL):
                a, b = parts[2 * u:2 * u + 2]
                scale = live / pltpu.roll(jnp.where(lane < 64, b, a), 64, 1)
                lin[:, pl.ds(col[u], LANES)] = scale.astype(BF)
                mix[:, pl.ds(col[u], LANES)] = (jnp.where(lane < 64, a, b) * scale).astype(BF)
            heads = pl.ds(2 * UNROLL * step, 2 * UNROLL)
            pltpu.make_async_copy(pb.at[heads], x_h.at[block, heads], osem.at[3]).start()

        copies.append(out(4, mix, mix_h.at[block]))
        copies.append(out(5, lin, lin_h.at[block]))
        if loading:
            loads[1].wait()
        for r in row_parts(rows):
            after = h[r].astype(F32) + dot_nn(mix[r], wp[...])
            acc[r] = after
            aft[r] = after.astype(BF)
            nm[r] = (normalized(after)[0] * g2_ref[...]).astype(BF)
        copies.append(out(6, aft, aft_h.at[block]))
        copies.append(out(7, nm, nm_h.at[block]))

        def up(t):
            return dot_nn(nm[...], wu[:, t * FT:(t + 1) * FT])

        if loading:
            loads[2].wait()
            loads[3].wait()
        u = up(0)
        total = None
        for t in range(tiles):
            following = up(t + 1) if t + 1 < tiles else None
            value, slope = gelu_and_slope(u)
            cols = slice(t * FT, (t + 1) * FT)
            value = value.astype(BF)
            act[:, cols] = value
            gp[block, :, cols] = slope.astype(BF)
            if t == tiles // 2:
                part = slice(0, t * FT)
                pltpu.make_async_copy(act.at[:, part], act_h.at[block, :, part], osem.at[8]).start()
            term = dot_nn(value, wd[cols, :])
            total = term if total is None else total + term
            u = following
        part = slice(tiles // 2 * FT, hidden)
        pltpu.make_async_copy(act.at[:, part], act_h.at[block, :, part], osem.at[8]).start()
        result = (acc[...] + total).astype(BF)
        low[...] = result
        copies.append(out(9, low, out_h.at[block]))
        copies.append(out(10, low, o_h))
        pltpu.make_async_copy(act, act_h.at[block], osem.at[8]).wait()
        pltpu.make_async_copy(pb, x_h.at[block], osem.at[3]).wait()
        for copy in copies:
            copy.wait()

    if loading:

        @pl.when(section != stage)
        def _():
            loads[0].wait()
            for copy in loads[1:]:
                copy.start()
            for copy in loads[1:]:
                copy.wait()


def estimate(flops):
    return pl.CostEstimate(flops=flops, bytes_accessed=30 << 20, transcendentals=0)


def held_shapes(weights):
    rows, hidden = MB_ROWS, weights[2].shape[-1]
    return [pltpu.VMEM(w.shape[-2:], BF) for w in weights[:4]] + [pltpu.VMEM((2, rows, hidden), BF)]


def forward(block, stage, h, video, view, g1, g2, held, kept):
    rows, width, hidden = MB_ROWS, h.shape[1], held[2].shape[-1]
    shapes = kept_shapes(rows, width, hidden)
    n = len(shapes)
    threaded = kept is not None
    outs = pl.pallas_call(
        functools.partial(forward_kernel, 2, 512, block, stage),
        out_shape=held_shapes(held)
        + [jax.ShapeDtypeStruct((rows, width), BF)]
        + [jax.ShapeDtypeStruct((2,) + s, d) for s, d in shapes],
        in_specs=[VM if stage else ANY] + [VM] * 4 + ([VM] * HELD + [ANY] * n if threaded else [ANY] * 4),
        out_specs=[VM] * HELD + [ANY] * (n + 1),
        scratch_shapes=[pltpu.VMEM(s, d) for s, d in shapes]
        + [pltpu.VMEM((rows, width), F32)]
        + [pltpu.SemaphoreType.DMA, pltpu.SemaphoreType.DMA((4,)), pltpu.SemaphoreType.DMA((n + 1,))],
        input_output_aliases={5 + i: i + (i >= HELD) for i in range(HELD + n)} if threaded else {},
        compiler_params=pltpu.CompilerParams(vmem_limit_bytes=VMEM_LIMIT),
        cost_estimate=estimate(25_000_000_000),
        name="forward",
    )(h, video, view, g1, g2, *held, *(kept if threaded else ()))
    return outs[HELD], outs[:HELD], outs[HELD + 1:]


def backward_shapes(rows, width, hidden):
    return [
        ((rows, width), BF),
        ((rows, hidden), BF),
        ((rows, width), BF),
        ((rows, 3 * width), BF),
        ((16, width), F32),
        ((rows, width), BF),
    ]


def backward_kernel(UNROLL, FT, block, stage, do_h, g1_ref, g2_ref, *rest):
    n = len(backward_shapes(1, 1, 1))
    h_k, qkv_h, x_h, mix_h, lin_h, aft_h = rest[HELD:HELD + 6]
    rest = rest[HELD + 6 + (0 if (block, stage) == (0, 1) else n):]
    wq, wp, wu, wd, gp = rest[:HELD]
    sent_h = rest[HELD]
    rest = rest[HELD + 1:]
    do_k, dup_h, dpi_h, dqkv_h, gain_h, dh_h = rest[:n]
    do, dup, dpi, dqkv, gain, low = rest[n:2 * n]
    h, qkv, x, mix, lin, aft, dos, qt, ot, da, isem, osem = rest[2 * n:]
    rows, width = h.shape
    hidden = wu.shape[1]
    pairs = width // LANES
    tiles = hidden // FT

    @pl.when(lax.axis_index("section") == stage)
    def _():
        sources = (
            (do_h.at[pl.ds(block * rows, rows)] if stage else do_h, do),
            (aft_h.at[block], aft),
            (lin_h.at[block], lin),
            (mix_h.at[block], mix),
            (qkv_h.at[block], qkv),
            (x_h.at[block], x),
            (h_k.at[block], h),
        )
        loads = [pltpu.make_async_copy(a, b, isem.at[i]) for i, (a, b) in enumerate(sources)]
        for copy in loads:
            copy.start()

        def out(i, src, dst):
            copy = pltpu.make_async_copy(src, dst, osem.at[i])
            copy.start()
            return copy

        loads[0].wait()
        d_out = do[...]

        def down(t):
            return dot_nt(d_out, wd[t * FT:(t + 1) * FT, :])

        u = down(0)
        total = None
        for t in range(tiles):
            following = down(t + 1) if t + 1 < tiles else None
            cols = slice(t * FT, (t + 1) * FT)
            value = (u * gp[block, :, cols].astype(F32)).astype(BF)
            dup[:, cols] = value
            term = dot_nt(value, wu[:, cols])
            total = term if total is None else total + term
            u = following
        copies = [out(0, do, do_k.at[block]), out(1, dup, dup_h.at[block])]
        loads[1].wait()
        hat, inv = normalized(aft[...].astype(F32))
        gain[8:16] = folded_rows(total * hat)
        d_after = d_out.astype(F32) + norm_back(total * g2_ref[...], hat, inv)
        da[...] = d_after
        dpi[...] = d_after.astype(BF)
        copies.append(out(2, dpi, dpi_h.at[block]))
        lane = lax.broadcasted_iota(jnp.int32, (1, LANES), 1)
        row = lax.broadcasted_iota(jnp.int32, (LANES, LANES), 0)
        column = lax.broadcasted_iota(jnp.int32, (LANES, LANES), 1)
        across = jnp.where((row < 64) != (column < 64), -1.0, 0.0).astype(BF)
        for copy in loads[2:]:
            copy.wait()
        dos[...] = (dot_nt(dpi[...], wp[...]) * lin[...].astype(F32)).astype(BF)
        for p in range(pairs):
            cols = slice(p * LANES, (p + 1) * LANES)
            qt[cols] = qkv[:, cols].T
            ot[cols] = dos[:, cols].T

        @pl.loop(0, pairs // UNROLL)
        def _(step):
            pair = [step * UNROLL + u for u in range(UNROLL)]
            col = [pl.multiple_of(p * LANES, LANES) for p in pair]

            def row_sums(u):
                here = pl.ds(col[u], LANES)
                product = dos[:, here].astype(F32) * mix[:, here].astype(F32)
                high = product.astype(BF)
                lower = (product - high.astype(F32)).astype(BF)
                negated = dot_nn(high, across) + dot_nn(lower, across)
                high = negated.astype(BF)
                lower = (negated - high.astype(F32)).astype(BF)
                place = lane % 64
                return jnp.where(place == 0, high, jnp.where(place == 1, lower, jnp.zeros_like(high)))

            sums = [row_sums(u) for u in range(UNROLL)]

            def d_scaled(u, e):
                d_mix = dos[:, pl.ds(col[u], LANES)]
                v = qkv[:, pl.ds(2 * width + col[u], LANES)]
                return dot_nt(in_half(lane, e, d_mix, sums[u]), in_half(lane, e, v, jnp.ones_like(v)))

            items = [(u, e) for u in range(UNROLL) for e in (0, 1)]
            s = d_scaled(*items[0])
            results = []
            for i, (u, e) in enumerate(items):
                following = d_scaled(*items[i + 1]) if i + 1 < len(items) else None
                weights = x[2 * pair[u] + e]
                d_scores = (weights.astype(F32) * s).astype(BF)
                k = qkv[:, pl.ds(width + col[u], LANES)]
                d_query = dot_nn(d_scores, in_half(lane, e, k, jnp.zeros_like(k)))
                head = pl.ds(pl.multiple_of(col[u] + 64 * e, 64), 64)
                results.append((d_query, dot_nn(qt[head], d_scores), dot_nn(ot[head], weights)))
                s = following
            for u in range(UNROLL):
                a, b = results[2 * u:2 * u + 2]
                dqkv[:, pl.ds(col[u], LANES)] = ((a[0] + b[0]) * 0.125).astype(BF)
                d_key = jnp.concatenate([a[1], b[1]], axis=0) * 0.125
                dqkv[:, pl.ds(width + col[u], LANES)] = d_key.astype(BF).T
                d_value = jnp.concatenate([a[2], b[2]], axis=0)
                dqkv[:, pl.ds(2 * width + col[u], LANES)] = d_value.astype(BF).T

        copies.append(out(3, dqkv, dqkv_h.at[block]))
        total = None
        for t in range(3):
            cols = slice(t * width, (t + 1) * width)
            term = dot_nt(dqkv[:, cols], wq[:, cols])
            total = term if total is None else total + term
        hat, inv = normalized(h[...].astype(F32))
        gain[0:8] = folded_rows(total * hat)
        copies.append(out(4, gain, gain_h.at[block]))
        result = (da[...] + norm_back(total * g1_ref[...], hat, inv)).astype(BF)
        low[...] = result
        copies.append(out(5, low, dh_h.at[block]))
        copies.append(out(6, low, sent_h))
        for copy in copies:
            copy.wait()


def backward(block, stage, d_out, g1, g2, held, saved, kept):
    rows, width, hidden = MB_ROWS, d_out.shape[1], held[2].shape[-1]
    shapes = backward_shapes(rows, width, hidden)
    n = len(shapes)
    threaded = kept is not None
    h, xn, qkv, x, mix, lin, aft, nm, act, produced = saved
    ins = (h, qkv, x, mix, lin, aft)
    aliases = {3 + i: i for i in range(HELD)}
    if threaded:
        aliases.update({3 + HELD + len(ins) + i: HELD + 1 + i for i in range(n)})
    outs = pl.pallas_call(
        functools.partial(backward_kernel, 2, 512, block, stage),
        out_shape=held_shapes(held)
        + [jax.ShapeDtypeStruct((rows, width), BF)]
        + [jax.ShapeDtypeStruct((2,) + s, d) for s, d in shapes],
        in_specs=[ANY] + [VM] * (2 + HELD) + [ANY] * (len(ins) + (n if threaded else 0)),
        out_specs=[VM] * HELD + [ANY] * (n + 1),
        scratch_shapes=[pltpu.VMEM(s, d) for s, d in shapes]
        + [pltpu.VMEM(a.shape[1:], a.dtype) for a in ins]
        + [pltpu.VMEM((rows, width), BF), pltpu.VMEM((width, rows), BF), pltpu.VMEM((width, rows), BF)]
        + [pltpu.VMEM((rows, width), F32)]
        + [pltpu.SemaphoreType.DMA((len(ins) + 1,)), pltpu.SemaphoreType.DMA((n + 1,))],
        input_output_aliases=aliases,
        compiler_params=pltpu.CompilerParams(vmem_limit_bytes=VMEM_LIMIT),
        cost_estimate=estimate(28_000_000_000),
        name="backward",
    )(d_out, g1, g2, *held, *ins, *(kept if threaded else ()))
    return outs[HELD], outs[:HELD], outs[HELD + 1:]


def near_first(part):
    return part in (3, 7)


def place_of(shard, swapped):
    x, near, far = (shard >> 1) & 1, (shard >> 2) & 1, (shard >> 3) & 1
    return (near, 2 * far + x) if swapped else (x, 2 * near + far)


def gradients_kernel(units, parts, gain_ref, arrays, q_ref, p_ref, n_ref, u_ref, d_ref, *scratch):
    a, b, o, packed, got0, got1, got2, got3, isem, ssem, rsem, gains, gsem = scratch
    width = p_ref.shape[1]
    share = width // SHARDS
    tokens = a.shape[1] * a.shape[2]
    count = len(parts)
    index = lax.axis_index("dp")
    bits = [lax.rem(index // (1 << k), 2) for k in range(4)]

    def partner(k):
        return {"dp": index + (1 << k) * (1 - 2 * bits[k])}

    barrier = pltpu.get_barrier_semaphore()
    for k in range(4):
        pl.semaphore_signal(barrier, inc=1, device_id=partner(k), device_id_type=MESH)

    def loads(i):
        left, left_at, right, right_at = units[i][:4]
        from_left = arrays[left].at[:, :, pl.ds(left_at * width, width)]
        from_right = arrays[right].at[:, :, pl.ds(right_at * width, width)]
        return (
            pltpu.make_async_copy(from_left, a.at[i % 2], isem.at[0, i % 2]),
            pltpu.make_async_copy(from_right, b.at[i % 2], isem.at[1, i % 2]),
        )

    def rows_of(t):
        return pl.ds(t * share, share + (16 if t == count - 1 else 0))

    def order(t):
        return (0, 2, 3, 1) if near_first(t) else (0, 1, 2, 3)

    def send(t, stage):
        rows = rows_of(t)
        first, second, third = [bits[k] for k in order(t)[1:]]
        if stage == 0:
            src, dst = packed.at[1, :, :, rows], got0.at[:, :, rows]
        elif stage == 1:
            src, dst = packed.at[0, 1 - first, :, rows], got1.at[:, rows]
        elif stage == 2:
            src, dst = packed.at[0, first, pl.ds(2 * (1 - second), 2), rows], got2.at[:, rows]
        else:
            src, dst = packed.at[0, first, 2 * second + 1 - third, rows], got3.at[rows]
        return pltpu.make_async_remote_copy(
            src_ref=src,
            dst_ref=dst,
            send_sem=ssem.at[stage, t],
            recv_sem=rsem.at[stage, t],
            device_id=partner(order(t)[stage]),
            device_id_type=MESH,
        )

    def added(first, second, rows, ref, at):
        total = packed[0, first, second, rows].astype(F32) + ref[at + (rows,)].astype(F32)
        packed[0, first, second, rows] = total.astype(BF)

    def combine(t, stage):
        rows = rows_of(t)
        first, second, third = [bits[k] for k in order(t)[1:]]
        send(t, stage).wait_recv()
        if stage == 0:
            for i in range(2):

                @pl.loop(0, 4)
                def _(j):
                    added(i, j, rows, got0, (i, j))

        elif stage == 1:

            @pl.loop(0, 4)
            def _(j):
                added(first, j, rows, got1, (j,))

        else:
            for i in range(2):
                added(first, 2 * second + i, rows, got2, (i,))
        send(t, stage + 1).start()

    def finish(t):
        rows = rows_of(t)
        first, second, third = [bits[k] for k in order(t)[1:]]
        send(t, 3).wait_recv()
        total = packed[0, first, 2 * second + third, rows].astype(F32) + got3[rows].astype(F32)
        kind, at = parts[t]
        if kind == "down":
            d_ref[at * share:(at + 1) * share] = total
        elif kind == "up":
            u_ref[:, at * width:(at + 1) * width] = total
        elif kind == "qkv":
            q_ref[:, at * width:(at + 1) * width] = total
        else:
            p_ref[...] = total[:share]
            for d in range(SHARDS):

                @pl.when(index == d)
                def _():
                    n_ref[...] = total[share:, d * share:(d + 1) * share]


    def place(d, t):
        first, rest = place_of(d, near_first(t))
        return lax.rem(bits[0] + d % 2, 2), first, rest, slice(t * share, (t + 1) * share)

    def produce(i):
        for copy in loads(i):
            copy.wait()
        if i + 1 < len(units):
            for copy in loads(i + 1):
                copy.start()
        kind, at = units[i][4:]

        @pl.loop(0, width // 256)
        def _(step):
            lanes = pl.ds(pl.multiple_of(step * 256, 256), 256)
            tile = a[i % 2, :, :, lanes].reshape(tokens, 256)
            o[lanes, :] = dot_tn(tile, b[i % 2].reshape(tokens, width)).astype(BF)

        if kind == "down":
            for d in range(4 * at, 4 * at + 4):
                for s in range(4):
                    base = (d % 4 * 4 + s) * share
                    packed[place(d, parts.index(("down", s)))] = o[base:base + share]
        else:
            for d in range(SHARDS):
                packed[place(d, parts.index((kind, at)))] = o[d * share:(d + 1) * share]
        if kind == "proj":
            row = lax.broadcasted_iota(jnp.int32, (16, width), 0)
            pltpu.make_async_copy(gain_ref, gains, gsem).wait()
            both = gains[0] + gains[1]
            upper = jnp.sum(both[0:8], axis=0, keepdims=True)
            lower = jnp.sum(both[8:16], axis=0, keepdims=True)
            gain = jnp.where(row == 0, upper, jnp.where(row == 1, lower, 0.0)).astype(BF)
            for side in range(2):
                for d in range(SHARDS // 2):
                    packed[side, d // 4, d % 4, count * share:count * share + 16] = gain

    for copy in loads(0):
        copy.start()
    pltpu.make_async_copy(gain_ref, gains, gsem).start()
    pl.semaphore_wait(barrier, 4)
    ready = 0
    for step in range(count + 3 * LAG + 1):
        while ready < ([1, 2, 4, 6, 8, 9, 10, 11, 12] + [len(units)] * 40)[step]:
            produce(ready)
            ready += 1
        if step < count:
            send(step, 0).start()
        for stage, t in enumerate((step - 1, step - 1 - LAG, step - 1 - 2 * LAG)):
            if 0 <= t < count:
                combine(t, stage)
        if 0 <= step - 1 - 3 * LAG < count:
            finish(step - 1 - 3 * LAG)
    for t in range(count):
        for stage in range(4):
            send(t, stage).wait_send()


def gradients(act, d_branch, nm, d_up, xn, d_qkv, mix, d_proj_in, gains):
    rows, width = d_branch.shape[1:]
    hidden = act.shape[2]
    share = width // SHARDS
    arrays = (act, d_branch, nm, d_up, xn, d_qkv, mix, d_proj_in)
    n = len(arrays)
    up = [(2, 0, 3, j, "up", j) for j in range(4)]
    down = [(0, j, 1, 0, "down", j) for j in range(4)]
    qkv = [(4, 0, 5, j, "qkv", j) for j in range(3)]
    proj = [(6, 0, 7, 0, "proj", 0)]
    units = [up[0], up[1], down[0], up[2], down[1], up[3], down[2], qkv[0], down[3], qkv[1], qkv[2], proj[0]]
    parts = [u[4:] for u in up + qkv[:1] + down + qkv[1:] + proj]
    total = len(parts) * share + 16

    def kernel(*refs):
        gradients_kernel(units, parts, refs[n], refs[:n], *refs[n + 1:])

    return pl.pallas_call(
        kernel,
        out_shape=[
            jax.ShapeDtypeStruct((share, 3 * width), F32),
            jax.ShapeDtypeStruct((share, width), F32),
            jax.ShapeDtypeStruct((16, share), F32),
            jax.ShapeDtypeStruct((share, hidden), F32),
            jax.ShapeDtypeStruct((hidden // SHARDS, width), F32),
        ],
        in_specs=[ANY] * (n + 1),
        out_specs=[VM] * 5,
        scratch_shapes=[
            pltpu.VMEM((2, 2, rows, width), BF),
            pltpu.VMEM((2, 2, rows, width), BF),
            pltpu.VMEM((width, width), BF),
            pltpu.VMEM((2, 2, 4, total, width), BF),
            pltpu.VMEM((2, 4, total, width), BF),
            pltpu.VMEM((4, total, width), BF),
            pltpu.VMEM((2, total, width), BF),
            pltpu.VMEM((total, width), BF),
            pltpu.SemaphoreType.DMA((2, 2)),
            pltpu.SemaphoreType.DMA((4, len(parts))),
            pltpu.SemaphoreType.DMA((4, len(parts))),
            pltpu.VMEM((2, 16, width), F32),
            pltpu.SemaphoreType.DMA,
        ],
        compiler_params=pltpu.CompilerParams(vmem_limit_bytes=50 << 20, collective_id=0, has_side_effects=True),
        cost_estimate=estimate(60_000_000_000),
        name="gradients",
    )(*arrays, gains)


def over_tokens(left, right):
    grad = lax.dot_general(left, right, (((0, 1), (0, 1)), ((), ())), preferred_element_type=F32)
    return grad.astype(BF)


def swap(value, bit, count):
    return lax.ppermute(value, "dp", [(i, i ^ bit) for i in range(count)])


def halving_sum(grad, count):
    index = lax.axis_index("dp")
    bit = 1
    while bit < count:
        mine = (index // bit) % 2
        pieces = grad.reshape((grad.shape[0] // 2, 2) + grad.shape[1:])
        sent = lax.dynamic_index_in_dim(pieces, 1 - mine, 1, keepdims=False)
        held = lax.dynamic_index_in_dim(pieces, mine, 1, keepdims=False)
        total = held.astype(F32) + swap(sent, bit, count).astype(F32)
        bit *= 2
        grad = total if bit == count else total.astype(BF)
    return grad[0]


def scattered(grad, count):
    return halving_sum(grad.reshape((count, grad.shape[0] // count) + grad.shape[1:]), count)


def on_device(inputs, video_ids, view_ids, attn_gain, mlp_gain, w_qkv, w_proj, w_up, w_down, out_grad):
    count = lax.axis_size("dp")
    rows, width = inputs.shape
    held = (w_qkv, w_proj, w_up, w_down)
    video, view = video_ids.reshape(1, rows), view_ids.reshape(1, rows)
    gains = (attn_gain, mlp_gain)

    saved = None
    arrived = []
    for block in (0, 1):
        out, held, saved = forward(block, 0, inputs, video, view, *gains, held, saved)
        arrived.append(lax.ppermute(out, "section", [(0, 1)]))
    for block in (0, 1):
        _, held, saved = forward(block, 1, arrived[block], video, view, *gains, held, saved)
    kept = None
    came = []
    for block in (0, 1):
        d_in, held, kept = backward(block, 1, out_grad, *gains, held, saved, kept)
        came.append(lax.ppermute(d_in, "section", [(1, 0)]))
    for block in (0, 1):
        _, held, kept = backward(block, 0, came[block], *gains, held, saved, kept)
    h, xn, qkv, x, mix, lin, aft, nm, act, layer_outputs = saved
    d_branch, d_up, d_proj_in, d_qkv, gain_grads, input_grads = kept

    hidden = w_up.shape[2]
    share = width // count
    if count == SHARDS and hidden == 4 * width:
        g_qkv, g_proj, gain_rows, g_up, g_down = gradients(
            act, d_branch, nm, d_up, xn, d_qkv, mix, d_proj_in, gain_grads
        )
        gain_sums = gain_rows[:2]
    else:
        g_down = scattered(over_tokens(act, d_branch), count)
        g_up = scattered(over_tokens(nm, d_up), count)
        g_proj = over_tokens(mix, d_proj_in).reshape(count, share, width)
        g_qkv = scattered(over_tokens(xn, d_qkv), count)
        gain_sums = gain_grads.reshape(2, 2, 8, width).sum((0, 2)).reshape(2, count, share)
        gain_sums = jnp.pad(gain_sums.transpose(1, 0, 2), ((0, 0), (0, 14), (0, width - share))).astype(BF)
        joined = halving_sum(jnp.concatenate([g_proj, gain_sums], axis=1), count)
        g_proj, gain_sums = joined[:share], joined[share:share + 2, :share]
    return (
        layer_outputs.reshape(1, rows, width),
        input_grads.reshape(1, rows, width),
        gain_sums[0:1],
        gain_sums[1:2],
        g_qkv[None],
        g_proj[None],
        g_up[None],
        g_down[None],
    )


def solution(mesh):
    in_specs = (
        P("dp", None),
        P("dp"),
        P("dp"),
        P("section", None),
        P("section", None),
        P("section", None, None),
        P("section", None, None),
        P("section", None, None),
        P("section", None, None),
        P("dp", None),
    )
    out_specs = (
        P("section", "dp", None),
        P("section", "dp", None),
        P("section", "dp"),
        P("section", "dp"),
        P("section", "dp", None),
        P("section", "dp", None),
        P("section", "dp", None),
        P("section", "dp", None),
    )
    return jax.shard_map(on_device, mesh=mesh, in_specs=in_specs, out_specs=out_specs, check_vma=False)
```

```python
import functools

import jax
import jax.numpy as jnp
from jax import lax
from jax.experimental import pallas as pl
from jax.experimental.pallas import tpu as pltpu
from jax.sharding import PartitionSpec as P

BF = jnp.bfloat16
F32 = jnp.float32
HEAD_DIM = 64
MB_ROWS = 512
EPSILON = 1e-6
NEG_FILL = -1e30
C0 = 0.7978845608028654
C1 = 0.044715
LANES = 128
VMEM_LIMIT = 43 << 20
HELD = 5
SHARDS = 16
LAG = 2
ROW_PART = 256

VM = pl.BlockSpec(memory_space=pltpu.VMEM)
ANY = pl.BlockSpec(memory_space=pl.ANY)
MESH = pl.DeviceIdType.MESH


def dot_nn(a, b):
    return jnp.dot(a, b, preferred_element_type=F32)


def dot_nt(a, b):
    return lax.dot_general(a, b, (((1,), (1,)), ((), ())), preferred_element_type=F32)


def dot_tn(a, b):
    return lax.dot_general(a, b, (((0,), (0,)), ((), ())), preferred_element_type=F32)


def normalized(x):
    center = x - jnp.mean(x, axis=-1, keepdims=True)
    inv = lax.rsqrt(jnp.mean(center * center, axis=-1, keepdims=True) + EPSILON)
    return center * inv, inv


def norm_back(d_hat, hat, inv):
    first = jnp.mean(d_hat, axis=-1, keepdims=True)
    second = jnp.mean(d_hat * hat, axis=-1, keepdims=True)
    return inv * (d_hat - first - hat * second)


def folded_rows(x):
    rows, width = x.shape
    return jnp.sum(x.reshape(rows // 8, 8, width), axis=0)


def row_parts(rows):
    return [slice(i * ROW_PART, (i + 1) * ROW_PART) for i in range(rows // ROW_PART)]


def gelu_and_slope(u):
    a = C0 * u
    b = a * (C1 * (u * u))
    gate = 0.5 + 0.5 * jnp.tanh(a + b)
    return u * gate, gate + (gate - gate * gate) * (2.0 * a + 6.0 * b)


def in_half(lane, half, inside, outside):
    return jnp.where((lane < 64) if half == 0 else (lane >= 64), inside, outside)


def kept_shapes(rows, width, hidden):
    heads = width // HEAD_DIM
    shapes = [
        ((rows, width), BF),
        ((rows, width), BF),
        ((rows, 3 * width), BF),
        ((heads, rows, rows), BF),
        ((rows, width), BF),
        ((rows, width), BF),
        ((rows, width), BF),
        ((rows, width), BF),
        ((rows, hidden), BF),
        ((rows, width), BF),
    ]
    return shapes


def forward_kernel(UNROLL, FT, block, stage, h_h, vid_ref, view_ref, g1_ref, g2_ref, *rest):
    count = len(kept_shapes(1, HEAD_DIM, 1))
    loading = (block, stage) == (0, 0)
    sources = rest[:4]
    rest = rest[4 if loading else HELD + count:]
    wq, wp, wu, wd, gp = rest[:HELD]
    o_h = rest[HELD]
    rest = rest[1 + HELD:]
    h_k, xn_h, qkv_h, x_h, mix_h, lin_h, aft_h, nm_h, act_h, out_h = rest[:count]
    h, xn, qkv, pb, mix, lin, aft, nm, act, low = rest[count:2 * count]
    acc, isem, wsem, osem = rest[2 * count:]
    rows, width = h.shape
    hidden = wu.shape[1]
    pairs = width // LANES
    section = lax.axis_index("section")
    if stage == 1:
        h = h_h
    loads = []
    if loading:
        loads = [pltpu.make_async_copy(a.at[0], b, wsem.at[i]) for i, (a, b) in enumerate(zip(sources, (wq, wp, wu, wd)))]
        loads[0].start()

    @pl.when(section == stage)
    def _():
        fetch = None
        if stage == 0:
            fetch = pltpu.make_async_copy(h_h.at[pl.ds(block * rows, rows)], h, isem)
            fetch.start()

        def out(i, src, dst):
            copy = pltpu.make_async_copy(src, dst, osem.at[i])
            copy.start()
            return copy

        here = pl.ds(block * rows, rows)
        video = vid_ref[:, here]
        view = view_ref[:, here]
        code = (video - video[:, :1]) * 4 + view
        place = lax.broadcasted_iota(jnp.int32, (LANES, rows), 0) % 64
        query_code = jnp.where(place == code - section, 1.0, 0.0).astype(BF).T
        key_code = jnp.where((place == code) | (place >= 8), 0.0, NEG_FILL).astype(BF).T
        live = jnp.broadcast_to(jnp.where(view >= section, 1.0, 0.0), (LANES, rows)).T
        if stage == 0:
            fetch.wait()
        if loading:
            loads[0].wait()
            for copy in loads[1:]:
                copy.start()
        for r in row_parts(rows):
            xn[r] = (normalized(h[r].astype(F32))[0] * g1_ref[...]).astype(BF)
            for t in range(3):
                cols = slice(t * width, (t + 1) * width)
                qkv[r, cols] = dot_nn(xn[r], wq[:, cols]).astype(BF)
        copies = [out(1, xn, xn_h.at[block])]
        copies.append(out(2, qkv, qkv_h.at[block]))
        tiles = hidden // FT
        copies.append(out(0, h, h_k.at[block]))
        lane = lax.broadcasted_iota(jnp.int32, (1, LANES), 1)

        @pl.loop(0, pairs // UNROLL)
        def _(step):
            pair = [step * UNROLL + u for u in range(UNROLL)]
            col = [pl.multiple_of(p * LANES, LANES) for p in pair]

            def scores(u, e):
                q = qkv[:, pl.ds(col[u], LANES)] * jnp.asarray(0.125, BF)
                k = qkv[:, pl.ds(width + col[u], LANES)]
                return dot_nt(in_half(lane, e, q, query_code), in_half(lane, e, k, key_code))

            def mixed(u, e, s):
                top = jnp.max(s, axis=-1, keepdims=True)
                x = jnp.exp(s - top).astype(BF)
                pb[2 * pair[u] + e] = x
                v = qkv[:, pl.ds(2 * width + col[u], LANES)]
                return dot_nn(x, in_half(lane, e, v, jnp.ones_like(v)))

            items = [(u, e) for u in range(UNROLL) for e in (0, 1)]
            s = scores(*items[0])
            parts = []
            for i, (u, e) in enumerate(items):
                following = scores(*items[i + 1]) if i + 1 < len(items) else None
                parts.append(mixed(u, e, s))
                s = following
            for u in range(UNROLL):
                a, b = parts[2 * u:2 * u + 2]
                scale = live / pltpu.roll(jnp.where(lane < 64, b, a), 64, 1)
                lin[:, pl.ds(col[u], LANES)] = scale.astype(BF)
                mix[:, pl.ds(col[u], LANES)] = (jnp.where(lane < 64, a, b) * scale).astype(BF)
            heads = pl.ds(2 * UNROLL * step, 2 * UNROLL)
            pltpu.make_async_copy(pb.at[heads], x_h.at[block, heads], osem.at[3]).start()

        copies.append(out(4, mix, mix_h.at[block]))
        copies.append(out(5, lin, lin_h.at[block]))
        if loading:
            loads[1].wait()
        for r in row_parts(rows):
            after = h[r].astype(F32) + dot_nn(mix[r], wp[...])
            acc[r] = after
            aft[r] = after.astype(BF)
            nm[r] = (normalized(after)[0] * g2_ref[...]).astype(BF)
        copies.append(out(6, aft, aft_h.at[block]))
        copies.append(out(7, nm, nm_h.at[block]))

        def up(t):
            return dot_nn(nm[...], wu[:, t * FT:(t + 1) * FT])

        if loading:
            loads[2].wait()
            loads[3].wait()
        u = up(0)
        total = None
        for t in range(tiles):
            following = up(t + 1) if t + 1 < tiles else None
            value, slope = gelu_and_slope(u)
            cols = slice(t * FT, (t + 1) * FT)
            value = value.astype(BF)
            act[:, cols] = value
            gp[block, :, cols] = slope.astype(BF)
            if t == tiles // 2:
                part = slice(0, t * FT)
                pltpu.make_async_copy(act.at[:, part], act_h.at[block, :, part], osem.at[8]).start()
            term = dot_nn(value, wd[cols, :])
            total = term if total is None else total + term
            u = following
        part = slice(tiles // 2 * FT, hidden)
        pltpu.make_async_copy(act.at[:, part], act_h.at[block, :, part], osem.at[8]).start()
        result = (acc[...] + total).astype(BF)
        low[...] = result
        copies.append(out(9, low, out_h.at[block]))
        copies.append(out(10, low, o_h))
        pltpu.make_async_copy(act, act_h.at[block], osem.at[8]).wait()
        pltpu.make_async_copy(pb, x_h.at[block], osem.at[3]).wait()
        for copy in copies:
            copy.wait()

    if loading:

        @pl.when(section != stage)
        def _():
            loads[0].wait()
            for copy in loads[1:]:
                copy.start()
            for copy in loads[1:]:
                copy.wait()


def estimate(flops):
    return pl.CostEstimate(flops=flops, bytes_accessed=30 << 20, transcendentals=0)


def held_shapes(weights):
    rows, hidden = MB_ROWS, weights[2].shape[-1]
    return [pltpu.VMEM(w.shape[-2:], BF) for w in weights[:4]] + [pltpu.VMEM((2, rows, hidden), BF)]


def forward(block, stage, h, video, view, g1, g2, held, kept):
    rows, width, hidden = MB_ROWS, h.shape[1], held[2].shape[-1]
    shapes = kept_shapes(rows, width, hidden)
    n = len(shapes)
    threaded = kept is not None
    outs = pl.pallas_call(
        functools.partial(forward_kernel, 2, 512, block, stage),
        out_shape=held_shapes(held)
        + [jax.ShapeDtypeStruct((rows, width), BF)]
        + [jax.ShapeDtypeStruct((2,) + s, d) for s, d in shapes],
        in_specs=[VM if stage else ANY] + [VM] * 4 + ([VM] * HELD + [ANY] * n if threaded else [ANY] * 4),
        out_specs=[VM] * HELD + [ANY] * (n + 1),
        scratch_shapes=[pltpu.VMEM(s, d) for s, d in shapes]
        + [pltpu.VMEM((rows, width), F32)]
        + [pltpu.SemaphoreType.DMA, pltpu.SemaphoreType.DMA((4,)), pltpu.SemaphoreType.DMA((n + 1,))],
        input_output_aliases={5 + i: i + (i >= HELD) for i in range(HELD + n)} if threaded else {},
        compiler_params=pltpu.CompilerParams(vmem_limit_bytes=VMEM_LIMIT),
        cost_estimate=estimate(25_000_000_000),
        name="forward",
    )(h, video, view, g1, g2, *held, *(kept if threaded else ()))
    return outs[HELD], outs[:HELD], outs[HELD + 1:]


def backward_shapes(rows, width, hidden):
    return [
        ((rows, width), BF),
        ((rows, hidden), BF),
        ((rows, width), BF),
        ((rows, 3 * width), BF),
        ((16, width), F32),
        ((rows, width), BF),
    ]


def backward_kernel(UNROLL, FT, block, stage, do_h, g1_ref, g2_ref, *rest):
    n = len(backward_shapes(1, 1, 1))
    h_k, qkv_h, x_h, mix_h, lin_h, aft_h = rest[HELD:HELD + 6]
    rest = rest[HELD + 6 + (0 if (block, stage) == (0, 1) else n):]
    wq, wp, wu, wd, gp = rest[:HELD]
    sent_h = rest[HELD]
    rest = rest[HELD + 1:]
    do_k, dup_h, dpi_h, dqkv_h, gain_h, dh_h = rest[:n]
    do, dup, dpi, dqkv, gain, low = rest[n:2 * n]
    h, qkv, x, mix, lin, aft, dos, qt, ot, da, isem, osem = rest[2 * n:]
    rows, width = h.shape
    hidden = wu.shape[1]
    pairs = width // LANES
    tiles = hidden // FT

    @pl.when(lax.axis_index("section") == stage)
    def _():
        sources = (
            (do_h.at[pl.ds(block * rows, rows)] if stage else do_h, do),
            (aft_h.at[block], aft),
            (lin_h.at[block], lin),
            (mix_h.at[block], mix),
            (qkv_h.at[block], qkv),
            (x_h.at[block], x),
            (h_k.at[block], h),
        )
        loads = [pltpu.make_async_copy(a, b, isem.at[i]) for i, (a, b) in enumerate(sources)]
        for copy in loads:
            copy.start()

        def out(i, src, dst):
            copy = pltpu.make_async_copy(src, dst, osem.at[i])
            copy.start()
            return copy

        loads[0].wait()
        d_out = do[...]

        def down(t):
            return dot_nt(d_out, wd[t * FT:(t + 1) * FT, :])

        u = down(0)
        total = None
        for t in range(tiles):
            following = down(t + 1) if t + 1 < tiles else None
            cols = slice(t * FT, (t + 1) * FT)
            value = (u * gp[block, :, cols].astype(F32)).astype(BF)
            dup[:, cols] = value
            term = dot_nt(value, wu[:, cols])
            total = term if total is None else total + term
            u = following
        copies = [out(0, do, do_k.at[block]), out(1, dup, dup_h.at[block])]
        loads[1].wait()
        hat, inv = normalized(aft[...].astype(F32))
        gain[8:16] = folded_rows(total * hat)
        d_after = d_out.astype(F32) + norm_back(total * g2_ref[...], hat, inv)
        da[...] = d_after
        dpi[...] = d_after.astype(BF)
        copies.append(out(2, dpi, dpi_h.at[block]))
        lane = lax.broadcasted_iota(jnp.int32, (1, LANES), 1)
        row = lax.broadcasted_iota(jnp.int32, (LANES, LANES), 0)
        column = lax.broadcasted_iota(jnp.int32, (LANES, LANES), 1)
        across = jnp.where((row < 64) != (column < 64), -1.0, 0.0).astype(BF)
        for copy in loads[2:]:
            copy.wait()
        dos[...] = (dot_nt(dpi[...], wp[...]) * lin[...].astype(F32)).astype(BF)
        for p in range(pairs):
            cols = slice(p * LANES, (p + 1) * LANES)
            qt[cols] = qkv[:, cols].T
            ot[cols] = dos[:, cols].T

        @pl.loop(0, pairs // UNROLL)
        def _(step):
            pair = [step * UNROLL + u for u in range(UNROLL)]
            col = [pl.multiple_of(p * LANES, LANES) for p in pair]

            def row_sums(u):
                here = pl.ds(col[u], LANES)
                product = dos[:, here].astype(F32) * mix[:, here].astype(F32)
                high = product.astype(BF)
                lower = (product - high.astype(F32)).astype(BF)
                negated = dot_nn(high, across) + dot_nn(lower, across)
                high = negated.astype(BF)
                lower = (negated - high.astype(F32)).astype(BF)
                place = lane % 64
                return jnp.where(place == 0, high, jnp.where(place == 1, lower, jnp.zeros_like(high)))

            sums = [row_sums(u) for u in range(UNROLL)]

            def d_scaled(u, e):
                d_mix = dos[:, pl.ds(col[u], LANES)]
                v = qkv[:, pl.ds(2 * width + col[u], LANES)]
                return dot_nt(in_half(lane, e, d_mix, sums[u]), in_half(lane, e, v, jnp.ones_like(v)))

            items = [(u, e) for u in range(UNROLL) for e in (0, 1)]
            s = d_scaled(*items[0])
            results = []
            for i, (u, e) in enumerate(items):
                following = d_scaled(*items[i + 1]) if i + 1 < len(items) else None
                weights = x[2 * pair[u] + e]
                d_scores = (weights.astype(F32) * s).astype(BF)
                k = qkv[:, pl.ds(width + col[u], LANES)]
                d_query = dot_nn(d_scores, in_half(lane, e, k, jnp.zeros_like(k)))
                head = pl.ds(pl.multiple_of(col[u] + 64 * e, 64), 64)
                results.append((d_query, dot_nn(qt[head], d_scores), dot_nn(ot[head], weights)))
                s = following
            for u in range(UNROLL):
                a, b = results[2 * u:2 * u + 2]
                dqkv[:, pl.ds(col[u], LANES)] = ((a[0] + b[0]) * 0.125).astype(BF)
                d_key = jnp.concatenate([a[1], b[1]], axis=0) * 0.125
                dqkv[:, pl.ds(width + col[u], LANES)] = d_key.astype(BF).T
                d_value = jnp.concatenate([a[2], b[2]], axis=0)
                dqkv[:, pl.ds(2 * width + col[u], LANES)] = d_value.astype(BF).T

        copies.append(out(3, dqkv, dqkv_h.at[block]))
        total = None
        for t in range(3):
            cols = slice(t * width, (t + 1) * width)
            term = dot_nt(dqkv[:, cols], wq[:, cols])
            total = term if total is None else total + term
        hat, inv = normalized(h[...].astype(F32))
        gain[0:8] = folded_rows(total * hat)
        copies.append(out(4, gain, gain_h.at[block]))
        result = (da[...] + norm_back(total * g1_ref[...], hat, inv)).astype(BF)
        low[...] = result
        copies.append(out(5, low, dh_h.at[block]))
        copies.append(out(6, low, sent_h))
        for copy in copies:
            copy.wait()


def backward(block, stage, d_out, g1, g2, held, saved, kept):
    rows, width, hidden = MB_ROWS, d_out.shape[1], held[2].shape[-1]
    shapes = backward_shapes(rows, width, hidden)
    n = len(shapes)
    threaded = kept is not None
    h, xn, qkv, x, mix, lin, aft, nm, act, produced = saved
    ins = (h, qkv, x, mix, lin, aft)
    aliases = {3 + i: i for i in range(HELD)}
    if threaded:
        aliases.update({3 + HELD + len(ins) + i: HELD + 1 + i for i in range(n)})
    outs = pl.pallas_call(
        functools.partial(backward_kernel, 2, 512, block, stage),
        out_shape=held_shapes(held)
        + [jax.ShapeDtypeStruct((rows, width), BF)]
        + [jax.ShapeDtypeStruct((2,) + s, d) for s, d in shapes],
        in_specs=[ANY] + [VM] * (2 + HELD) + [ANY] * (len(ins) + (n if threaded else 0)),
        out_specs=[VM] * HELD + [ANY] * (n + 1),
        scratch_shapes=[pltpu.VMEM(s, d) for s, d in shapes]
        + [pltpu.VMEM(a.shape[1:], a.dtype) for a in ins]
        + [pltpu.VMEM((rows, width), BF), pltpu.VMEM((width, rows), BF), pltpu.VMEM((width, rows), BF)]
        + [pltpu.VMEM((rows, width), F32)]
        + [pltpu.SemaphoreType.DMA((len(ins) + 1,)), pltpu.SemaphoreType.DMA((n + 1,))],
        input_output_aliases=aliases,
        compiler_params=pltpu.CompilerParams(vmem_limit_bytes=VMEM_LIMIT),
        cost_estimate=estimate(28_000_000_000),
        name="backward",
    )(d_out, g1, g2, *held, *ins, *(kept if threaded else ()))
    return outs[HELD], outs[:HELD], outs[HELD + 1:]


def near_first(part):
    return part in (3, 7)


def place_of(shard, swapped):
    x, near, far = (shard >> 1) & 1, (shard >> 2) & 1, (shard >> 3) & 1
    return (near, 2 * far + x) if swapped else (x, 2 * near + far)


def gradients_kernel(units, parts, gain_ref, arrays, q_ref, p_ref, n_ref, u_ref, d_ref, *scratch):
    a, b, o, packed, got0, got1, got2, got3, isem, ssem, rsem, gains, gsem = scratch
    width = p_ref.shape[1]
    share = width // SHARDS
    tokens = a.shape[1] * a.shape[2]
    count = len(parts)
    index = lax.axis_index("dp")
    bits = [lax.rem(index // (1 << k), 2) for k in range(4)]

    def partner(k):
        return {"dp": index + (1 << k) * (1 - 2 * bits[k])}

    barrier = pltpu.get_barrier_semaphore()
    for k in range(4):
        pl.semaphore_signal(barrier, inc=1, device_id=partner(k), device_id_type=MESH)

    def loads(i):
        left, left_at, right, right_at = units[i][:4]
        from_left = arrays[left].at[:, :, pl.ds(left_at * width, width)]
        from_right = arrays[right].at[:, :, pl.ds(right_at * width, width)]
        return (
            pltpu.make_async_copy(from_left, a.at[i % 2], isem.at[0, i % 2]),
            pltpu.make_async_copy(from_right, b.at[i % 2], isem.at[1, i % 2]),
        )

    def rows_of(t):
        return pl.ds(t * share, share + (16 if t == count - 1 else 0))

    def order(t):
        return (0, 2, 3, 1) if near_first(t) else (0, 1, 2, 3)

    def send(t, stage):
        rows = rows_of(t)
        first, second, third = [bits[k] for k in order(t)[1:]]
        if stage == 0:
            src, dst = packed.at[1, :, :, rows], got0.at[:, :, rows]
        elif stage == 1:
            src, dst = packed.at[0, 1 - first, :, rows], got1.at[:, rows]
        elif stage == 2:
            src, dst = packed.at[0, first, pl.ds(2 * (1 - second), 2), rows], got2.at[:, rows]
        else:
            src, dst = packed.at[0, first, 2 * second + 1 - third, rows], got3.at[rows]
        return pltpu.make_async_remote_copy(
            src_ref=src,
            dst_ref=dst,
            send_sem=ssem.at[stage, t],
            recv_sem=rsem.at[stage, t],
            device_id=partner(order(t)[stage]),
            device_id_type=MESH,
        )

    def added(first, second, rows, ref, at):
        total = packed[0, first, second, rows].astype(F32) + ref[at + (rows,)].astype(F32)
        packed[0, first, second, rows] = total.astype(BF)

    def combine(t, stage):
        rows = rows_of(t)
        first, second, third = [bits[k] for k in order(t)[1:]]
        send(t, stage).wait_recv()
        if stage == 0:
            for i in range(2):

                @pl.loop(0, 4)
                def _(j):
                    added(i, j, rows, got0, (i, j))

        elif stage == 1:

            @pl.loop(0, 4)
            def _(j):
                added(first, j, rows, got1, (j,))

        else:
            for i in range(2):
                added(first, 2 * second + i, rows, got2, (i,))
        send(t, stage + 1).start()

    def finish(t):
        rows = rows_of(t)
        first, second, third = [bits[k] for k in order(t)[1:]]
        send(t, 3).wait_recv()
        total = packed[0, first, 2 * second + third, rows].astype(F32) + got3[rows].astype(F32)
        kind, at = parts[t]
        if kind == "down":
            d_ref[at * share:(at + 1) * share] = total
        elif kind == "up":
            u_ref[:, at * width:(at + 1) * width] = total
        elif kind == "qkv":
            q_ref[:, at * width:(at + 1) * width] = total
        else:
            p_ref[...] = total[:share]
            for d in range(SHARDS):

                @pl.when(index == d)
                def _():
                    n_ref[...] = total[share:, d * share:(d + 1) * share]


    def place(d, t):
        first, rest = place_of(d, near_first(t))
        return lax.rem(bits[0] + d % 2, 2), first, rest, slice(t * share, (t + 1) * share)

    def produce(i):
        for copy in loads(i):
            copy.wait()
        if i + 1 < len(units):
            for copy in loads(i + 1):
                copy.start()
        kind, at = units[i][4:]

        @pl.loop(0, width // 256)
        def _(step):
            lanes = pl.ds(pl.multiple_of(step * 256, 256), 256)
            tile = a[i % 2, :, :, lanes].reshape(tokens, 256)
            o[lanes, :] = dot_tn(tile, b[i % 2].reshape(tokens, width)).astype(BF)

        if kind == "down":
            for d in range(4 * at, 4 * at + 4):
                for s in range(4):
                    base = (d % 4 * 4 + s) * share
                    packed[place(d, parts.index(("down", s)))] = o[base:base + share]
        else:
            for d in range(SHARDS):
                packed[place(d, parts.index((kind, at)))] = o[d * share:(d + 1) * share]
        if kind == "proj":
            row = lax.broadcasted_iota(jnp.int32, (16, width), 0)
            pltpu.make_async_copy(gain_ref, gains, gsem).wait()
            both = gains[0] + gains[1]
            upper = jnp.sum(both[0:8], axis=0, keepdims=True)
            lower = jnp.sum(both[8:16], axis=0, keepdims=True)
            gain = jnp.where(row == 0, upper, jnp.where(row == 1, lower, 0.0)).astype(BF)
            for side in range(2):
                for d in range(SHARDS // 2):
                    packed[side, d // 4, d % 4, count * share:count * share + 16] = gain

    for copy in loads(0):
        copy.start()
    pltpu.make_async_copy(gain_ref, gains, gsem).start()
    pl.semaphore_wait(barrier, 4)
    ready = 0
    for step in range(count + 3 * LAG + 1):
        while ready < ([1, 2, 4, 6, 8, 9, 10, 11, 12] + [len(units)] * 40)[step]:
            produce(ready)
            ready += 1
        if step < count:
            send(step, 0).start()
        for stage, t in enumerate((step - 1, step - 1 - LAG, step - 1 - 2 * LAG)):
            if 0 <= t < count:
                combine(t, stage)
        if 0 <= step - 1 - 3 * LAG < count:
            finish(step - 1 - 3 * LAG)
    for t in range(count):
        for stage in range(4):
            send(t, stage).wait_send()


def gradients(act, d_branch, nm, d_up, xn, d_qkv, mix, d_proj_in, gains):
    rows, width = d_branch.shape[1:]
    hidden = act.shape[2]
    share = width // SHARDS
    arrays = (act, d_branch, nm, d_up, xn, d_qkv, mix, d_proj_in)
    n = len(arrays)
    up = [(2, 0, 3, j, "up", j) for j in range(4)]
    down = [(0, j, 1, 0, "down", j) for j in range(4)]
    qkv = [(4, 0, 5, j, "qkv", j) for j in range(3)]
    proj = [(6, 0, 7, 0, "proj", 0)]
    units = [up[0], up[1], down[0], up[2], down[1], up[3], down[2], qkv[0], down[3], qkv[1], qkv[2], proj[0]]
    parts = [u[4:] for u in up + qkv[:1] + down + qkv[1:] + proj]
    total = len(parts) * share + 16

    def kernel(*refs):
        gradients_kernel(units, parts, refs[n], refs[:n], *refs[n + 1:])

    return pl.pallas_call(
        kernel,
        out_shape=[
            jax.ShapeDtypeStruct((share, 3 * width), F32),
            jax.ShapeDtypeStruct((share, width), F32),
            jax.ShapeDtypeStruct((16, share), F32),
            jax.ShapeDtypeStruct((share, hidden), F32),
            jax.ShapeDtypeStruct((hidden // SHARDS, width), F32),
        ],
        in_specs=[ANY] * (n + 1),
        out_specs=[VM] * 5,
        scratch_shapes=[
            pltpu.VMEM((2, 2, rows, width), BF),
            pltpu.VMEM((2, 2, rows, width), BF),
            pltpu.VMEM((width, width), BF),
            pltpu.VMEM((2, 2, 4, total, width), BF),
            pltpu.VMEM((2, 4, total, width), BF),
            pltpu.VMEM((4, total, width), BF),
            pltpu.VMEM((2, total, width), BF),
            pltpu.VMEM((total, width), BF),
            pltpu.SemaphoreType.DMA((2, 2)),
            pltpu.SemaphoreType.DMA((4, len(parts))),
            pltpu.SemaphoreType.DMA((4, len(parts))),
            pltpu.VMEM((2, 16, width), F32),
            pltpu.SemaphoreType.DMA,
        ],
        compiler_params=pltpu.CompilerParams(vmem_limit_bytes=52 << 20, collective_id=0, has_side_effects=True),
        cost_estimate=estimate(60_000_000_000),
        name="gradients",
    )(*arrays, gains)


def over_tokens(left, right):
    grad = lax.dot_general(left, right, (((0, 1), (0, 1)), ((), ())), preferred_element_type=F32)
    return grad.astype(BF)


def swap(value, bit, count):
    return lax.ppermute(value, "dp", [(i, i ^ bit) for i in range(count)])


def halving_sum(grad, count):
    index = lax.axis_index("dp")
    bit = 1
    while bit < count:
        mine = (index // bit) % 2
        pieces = grad.reshape((grad.shape[0] // 2, 2) + grad.shape[1:])
        sent = lax.dynamic_index_in_dim(pieces, 1 - mine, 1, keepdims=False)
        held = lax.dynamic_index_in_dim(pieces, mine, 1, keepdims=False)
        total = held.astype(F32) + swap(sent, bit, count).astype(F32)
        bit *= 2
        grad = total if bit == count else total.astype(BF)
    return grad[0]


def scattered(grad, count):
    return halving_sum(grad.reshape((count, grad.shape[0] // count) + grad.shape[1:]), count)


def on_device(inputs, video_ids, view_ids, attn_gain, mlp_gain, w_qkv, w_proj, w_up, w_down, out_grad):
    count = lax.axis_size("dp")
    rows, width = inputs.shape
    held = (w_qkv, w_proj, w_up, w_down)
    video, view = video_ids.reshape(1, rows), view_ids.reshape(1, rows)
    gains = (attn_gain, mlp_gain)

    saved = None
    arrived = []
    for block in (0, 1):
        out, held, saved = forward(block, 0, inputs, video, view, *gains, held, saved)
        arrived.append(lax.ppermute(out, "section", [(0, 1)]))
    for block in (0, 1):
        _, held, saved = forward(block, 1, arrived[block], video, view, *gains, held, saved)
    kept = None
    came = []
    for block in (0, 1):
        d_in, held, kept = backward(block, 1, out_grad, *gains, held, saved, kept)
        came.append(lax.ppermute(d_in, "section", [(1, 0)]))
    for block in (0, 1):
        _, held, kept = backward(block, 0, came[block], *gains, held, saved, kept)
    h, xn, qkv, x, mix, lin, aft, nm, act, layer_outputs = saved
    d_branch, d_up, d_proj_in, d_qkv, gain_grads, input_grads = kept

    hidden = w_up.shape[2]
    share = width // count
    if count == SHARDS and hidden == 4 * width:
        g_qkv, g_proj, gain_rows, g_up, g_down = gradients(
            act, d_branch, nm, d_up, xn, d_qkv, mix, d_proj_in, gain_grads
        )
        gain_sums = gain_rows[:2]
    else:
        g_down = scattered(over_tokens(act, d_branch), count)
        g_up = scattered(over_tokens(nm, d_up), count)
        g_proj = over_tokens(mix, d_proj_in).reshape(count, share, width)
        g_qkv = scattered(over_tokens(xn, d_qkv), count)
        gain_sums = gain_grads.reshape(2, 2, 8, width).sum((0, 2)).reshape(2, count, share)
        gain_sums = jnp.pad(gain_sums.transpose(1, 0, 2), ((0, 0), (0, 14), (0, width - share))).astype(BF)
        joined = halving_sum(jnp.concatenate([g_proj, gain_sums], axis=1), count)
        g_proj, gain_sums = joined[:share], joined[share:share + 2, :share]
    return (
        layer_outputs.reshape(1, rows, width),
        input_grads.reshape(1, rows, width),
        gain_sums[0:1],
        gain_sums[1:2],
        g_qkv[None],
        g_proj[None],
        g_up[None],
        g_down[None],
    )


def solution(mesh):
    in_specs = (
        P("dp", None),
        P("dp"),
        P("dp"),
        P("section", None),
        P("section", None),
        P("section", None, None),
        P("section", None, None),
        P("section", None, None),
        P("section", None, None),
        P("dp", None),
    )
    out_specs = (
        P("section", "dp", None),
        P("section", "dp", None),
        P("section", "dp"),
        P("section", "dp"),
        P("section", "dp", None),
        P("section", "dp", None),
        P("section", "dp", None),
        P("section", "dp", None),
    )
    return jax.shard_map(on_device, mesh=mesh, in_specs=in_specs, out_specs=out_specs, check_vma=False)
```
